32 devices in a mesh: pair: 2 (over core), vcol: 16 (over z, y, x).
Axes of the slice: x: 2, y: 2, z: 4, core: 2. Of those that a mesh axis runs over, the one named last changes fastest.
Arguments:
- amplitudes: bfloat16 [1280, 4096], P('pair', 'vcol'), may hold values from -6 to 6
- tile_owner: int32 [32], replicated, may hold values from 0 to 31, each once
- integrals: bfloat16 [4096, 4096], P('pair', 'vcol'), may hold values from -0.125 to 0.125
- screening: int32 [20, 32, 32], P('pair'), may hold values 0 or 1
- occ_energy: float32 [1280], P('pair'), may hold values from -1 to -0.2
- virt_energy: float32 [4096], replicated, may hold values from 0.2 to 1
Outputs:
- residual: bfloat16 [1280, 4096], P('pair', 'vcol')
The draws below stay inside these ranges and needn't reach their ends.
Inputs may be any that keep to these rules, and one draw needn't show every extreme that they name: `tile_owner`: each of the 32 tiles appears exactly once.
All inputs are finite; a program needn't handle non-finite values. No bound on the sum of `screening` on one device may be relied on, other than what follows from the above.
Results may differ from the reference program's by a relative error of at most 0.0036.
Values may be sent and summed in bfloat16 or wider, within the bound.
A program may use at most 64 MiB of HBM per device.

```python
import jax
import jax.numpy as jnp
from jax import lax

TILE = 128
PBLK = 64
PAIRS = 1280
KT = 32
K = 4096
NPB = 20


def plant(result, own_key, low, high):
    dims = result.shape
    index_at = [jax.random.randint(jax.random.fold_in(own_key, axis), (), 0, dims[axis]) for axis in range(len(dims))]
    result = result.at[tuple(index_at)].set(low)
    longest = dims.index(max(dims))
    index_at[longest] = (index_at[longest] + 1) % dims[longest]
    return result.at[tuple(index_at)].set(high)


def strengthened(result, own_key, source, target, shards_of, factor):
    owner, partner = [(jnp.arange(result.shape[dim]) // (result.shape[dim] // shards_of)).reshape([-1 if axis == dim else 1 for axis in range(result.ndim)]) for dim in (source, target)]
    chosen = jax.random.permutation(own_key, shards_of)[partner]
    strong = (owner == chosen) | (owner == (partner + shards_of // 2) % shards_of)
    return jnp.where(strong, factor * result, result)


def block_scale(rng, extent, pieces, smallest, top_value):
    loudness, own = 1.0, jax.random.fold_in(rng, 6)
    for dim, shards_of in pieces:
        draws = jnp.exp(jax.random.uniform(jax.random.fold_in(own, dim), (shards_of,), jnp.float32, smallest / len(pieces), top_value / len(pieces)))
        loudness = loudness * jnp.repeat(draws, extent[dim] // shards_of).reshape([-1 if axis == dim else 1 for axis in range(len(extent))])
    return loudness


def noise(stream_key, shape, scale, limit, cuts=(), kind=jnp.bfloat16):
    array = scale * jax.random.normal(stream_key, shape, jnp.float32)
    if cuts:
        array = array * block_scale(stream_key, shape, cuts, -0.22, 0.18)
    return jnp.clip(array, -limit, limit).astype(kind)


def heavy_noise(own_key, shape, deviation, reach, split, heavy, held_as=jnp.bfloat16):
    values = deviation * jax.random.normal(own_key, shape, jnp.float32)
    if split:
        values = values * block_scale(own_key, shape, split, -0.22, 0.18)
    return jnp.clip(strengthened(values, jax.random.fold_in(own_key, 3), *heavy), -reach, reach).astype(held_as)


def setup_inputs(seed: int = 0) -> dict:
    arg_keys = jax.random.split(jax.random.key(seed), 7)
    amplitudes = noise(arg_keys[0], (PAIRS, K), 1.0, 6.0, ((0, 2), (1, 16)))
    tile_owner = jax.random.permutation(arg_keys[1], KT).astype(jnp.int32)
    integrals = heavy_noise(arg_keys[2], (K, K), K ** -0.5, 0.125, ((0, 2), (1, 16)), (0, 1, 16, 2.0))
    screening = plant((jax.random.randint(arg_keys[3], (NPB, KT, KT), 0, 4) < 3).astype(jnp.int32), jax.random.fold_in(arg_keys[3], 1), 0, 1)
    occ_energy = jnp.clip(-1.0 + 0.8 * jax.random.uniform(arg_keys[4], (PAIRS,), jnp.float32) ** block_scale(arg_keys[4], (PAIRS,), ((0, 2),), -0.2, 0.2), -1.0, -0.2)
    virt_energy = jnp.clip(jax.random.uniform(arg_keys[5], (K,), jnp.float32, 0.2, 1.0), 0.2, 1.0)
    return {"amplitudes": amplitudes, "tile_owner": tile_owner, "integrals": integrals, "screening": screening, "occ_energy": occ_energy, "virt_energy": virt_energy}


def reference(amplitudes, tile_owner, integrals, screening, occ_energy, virt_energy):
    pair_count = amplitudes.shape[0]
    tile_count = tile_owner.shape[0]
    slot_tiles = amplitudes.reshape(pair_count, tile_count, TILE)
    natural = jnp.zeros_like(slot_tiles).at[:, tile_owner].set(slot_tiles).reshape(pair_count, tile_count * TILE)
    grid_ints = integrals.reshape(tile_count, TILE, tile_count, TILE)
    blocks = natural.reshape(pair_count // PBLK, PBLK, tile_count * TILE)

    def one_block(operands):
        left_rows, marks = operands
        masked = (grid_ints * marks.astype(grid_ints.dtype)[:, None, :, None]).reshape(tile_count * TILE, tile_count * TILE)
        return jnp.dot(left_rows, masked, preferred_element_type=jnp.float32)

    ladder = lax.map(one_block, (blocks, screening)).reshape(pair_count, tile_count * TILE).astype(jnp.bfloat16)
    owned_tiles = ladder.reshape(pair_count, tile_count, TILE)[:, tile_owner].reshape(pair_count, tile_count * TILE).astype(jnp.float32)
    virt_owned = virt_energy.reshape(tile_count, TILE)[tile_owner].reshape(tile_count * TILE)
    residual = owned_tiles + (virt_owned[None, :] - occ_energy[:, None]) * amplitudes.astype(jnp.float32)
    return residual.astype(jnp.bfloat16)
```

```python
import functools

import jax
import jax.numpy as jnp
from jax import lax
from jax.experimental import pallas as pl
from jax.experimental.pallas import tpu as pltpu
from jax.sharding import PartitionSpec as P

TILE = 128
PBLK = 64
KT_DEV = 2
MESH = pl.DeviceIdType.MESH
UP, DOWN, BESIDE, PARTNER = 0, 1, 2, 3


def one_hot(indices, length):
    return (indices[:, None] == jnp.arange(length, dtype=jnp.int32)[None, :]).astype(jnp.float32)


def ladder_kernel(
    ranks, pairs, owner, screen, amps, ints, out,
    gath, panel, stage, far, lhs, acc, parts, natural, slots, landed,
    local_sem, send_sem, recv_sem, pair_send, pair_recv, far_send, far_recv, pass_send, pass_recv,
    out_send, out_recv, back_send, back_recv,
):
    length = ranks // 4
    plane = ranks // 2
    me = lax.axis_index("vcol")
    core = lax.axis_index("pair")
    line, spot = me // 4, me % 4
    hi, lo = spot // 2, spot % 2
    beside = line * 4 + hi * 2 + (1 - lo)
    partner = line * 4 + (1 - hi) * 2 + lo
    has_up, has_down = line < length - 1, line > 0
    half = gath.shape[1]
    blocks = half // PBLK
    tiles = ints.shape[0]
    chunks = stage.shape[0]
    per_line = chunks // length

    own_amps = pltpu.make_async_copy(amps.at[pl.ds(hi * half, half)], gath.at[me], local_sem.at[0])
    own_ints = pltpu.make_async_copy(ints, panel.at[pl.ds(core * tiles, tiles)], local_sem.at[1])
    own_amps.start()
    own_ints.start()

    barrier = pltpu.get_barrier_semaphore()

    def greet_step(step, _):
        pl.semaphore_signal(
            barrier, inc=1, device_id={"vcol": (me + step) % ranks}, device_id_type=MESH
        )
        return 0

    lax.fori_loop(1, ranks, greet_step, 0)
    for step in range(1, pairs):
        pl.semaphore_signal(
            barrier, inc=1, device_id={"pair": (core + step) % pairs}, device_id_type=MESH
        )
    pl.semaphore_wait(barrier, ranks - 1 + pairs - 1)

    cut = (blocks * 3 // 5) * PBLK
    bands = ((0, cut), (cut, half))

    def first_copy(band, way, target):
        low, high = bands[band]
        base = (1 - hi) * half if way == PARTNER else hi * half
        return pltpu.make_async_remote_copy(
            src_ref=amps.at[pl.ds(base + low, high - low)],
            dst_ref=gath.at[me, pl.ds(low, high - low)],
            send_sem=send_sem.at[band, way, me], recv_sem=recv_sem.at[band, me],
            device_id={"vcol": target}, device_id_type=MESH,
        )

    def relay(source, band, way, target):
        low, high = bands[band]
        place = gath.at[source, pl.ds(low, high - low)]
        return pltpu.make_async_remote_copy(
            src_ref=place, dst_ref=place,
            send_sem=send_sem.at[band, way, source], recv_sem=recv_sem.at[band, source],
            device_id={"vcol": target}, device_id_type=MESH,
        )

    def arrived(source, band):
        relay(source, band, BESIDE, beside).wait_recv()

    def panel_copy(step):
        return pltpu.make_async_remote_copy(
            src_ref=ints, dst_ref=panel.at[pl.ds(core * tiles, tiles)],
            send_sem=pair_send.at[step - 1], recv_sem=pair_recv.at[step - 1],
            device_id={"pair": (core + step) % pairs}, device_id_type=MESH,
        )

    def far_copy(chunk):
        return pltpu.make_async_remote_copy(
            src_ref=stage.at[chunk], dst_ref=far.at[chunk * pairs + core],
            send_sem=far_send.at[chunk], recv_sem=far_recv.at[chunk],
            device_id={"vcol": partner}, device_id_type=MESH,
        )

    def pass_copy(chunk, step, holder):
        place = far.at[chunk * pairs + holder]
        return pltpu.make_async_remote_copy(
            src_ref=place, dst_ref=place,
            send_sem=pass_send.at[step - 1, chunk], recv_sem=pass_recv.at[step - 1, chunk],
            device_id={"pair": (core + step) % pairs}, device_id_type=MESH,
        )

    def multiply(source, side):
        tile_pair = (owner[KT_DEV * source], owner[KT_DEV * source + 1])
        home = partner if side else me
        for slot, tile in enumerate(tile_pair):
            columns = slice(slot * TILE, (slot + 1) * TILE)
            for block in range(blocks):
                part = slice(block * PBLK, (block + 1) * PBLK)
                value = gath[source, part, columns]
                for n in range(KT_DEV):
                    mark = screen[hi * blocks + block, tile, KT_DEV * home + n].astype(jnp.float32)
                    lhs[n, part, columns] = value * jnp.full(value.shape, mark, jnp.float32).astype(
                        value.dtype
                    )
        if side:
            right = jnp.concatenate([far[KT_DEV * source], far[KT_DEV * source + 1]], axis=0)
        else:
            right = jnp.concatenate([panel[tile] for tile in tile_pair], axis=0)
        for n in range(KT_DEV):
            columns = slice(n * TILE, (n + 1) * TILE)
            place = slice((KT_DEV * side + n) * TILE, (KT_DEV * side + n + 1) * TILE)
            acc[:, place] += jnp.dot(lhs[n], right[:, columns], preferred_element_type=jnp.float32)

    def offset(e):
        return ((e + 1) // 2) * (1 - 2 * (e % 2))

    def inside(e):
        at = line + offset(e)
        return (at >= 0) & (at < length)

    def goes_up(e):
        return ((e % 2 == 1) | (e == 0)) & has_up

    def goes_down(e):
        return (e % 2 == 0) & has_down

    def forward(source, band, e, action):
        @pl.when(goes_up(e))
        def _():
            action(relay(source, band, UP, me + 4))

        @pl.when(goes_down(e))
        def _():
            action(relay(source, band, DOWN, me - 4))

        action(relay(source, band, BESIDE, beside))

    def start(copy):
        copy.start()

    def wait_send(copy):
        copy.wait_send()

    def first_copies(action):
        for band in (0, 1):
            action(first_copy(band, PARTNER, partner))

            @pl.when(has_up)
            def _():
                action(first_copy(band, UP, me + 4))

            @pl.when(has_down)
            def _():
                action(first_copy(band, DOWN, me - 4))

            action(first_copy(band, BESIDE, beside))

    first_copies(start)
    for step in range(1, pairs):
        panel_copy(step).start()
    acc[...] = jnp.zeros_like(acc)
    own_ints.wait()
    for step in range(1, pairs):
        panel_copy(step).wait_recv()

    last = 2 * length - 1

    def on_line(e, action):
        @pl.when(inside(e))
        def _():
            for i in range(per_line):
                action((line + offset(e)) * per_line + i)

    def stage_line(e, _):
        def fill(chunk):
            stage[chunk] = panel[owner[chunk * pairs + core]]

        on_line(e, fill)
        return 0

    def send_line(e, _):
        on_line(e, lambda chunk: far_copy(chunk).start())
        return 0

    lax.fori_loop(0, last, stage_line, 0)
    lax.fori_loop(0, last, send_line, 0)
    for band in (0, 1):
        arrived(partner, band)
        forward(partner, band, jnp.int32(0), start)
    own_amps.wait()
    multiply(me, 0)
    multiply(partner, 0)

    def on_step(e, _):
        at = line + offset(e)

        @pl.when((e < last) & inside(e))
        def _():
            for h in (hi, 1 - hi):
                for band in (0, 1):
                    arrived(at * 4 + h * 2 + lo, band)
                    forward(at * 4 + h * 2 + lo, band, e, start)

        late = e - 2
        behind = line + offset(late)

        @pl.when((late >= 0) & inside(late))
        def _():
            for i in range(per_line):
                chunk = behind * per_line + i
                far_copy(chunk).wait_recv()
                for step in range(1, pairs):
                    pass_copy(chunk, step, core).start()

        @pl.when((e < last) & inside(e))
        def _():
            for h in range(2):
                multiply(at * 4 + h * 2 + lo, 0)

        @pl.when((late >= 0) & inside(late))
        def _():
            for h in (hi, 1 - hi):
                source = behind * 4 + h * 2 + (1 - lo)
                for band in (0, 1):
                    arrived(source, band)
                multiply(source, 0)
            for i in range(per_line):
                for step in range(1, pairs):
                    pass_copy(
                        behind * per_line + i, step, (core + pairs - step) % pairs
                    ).wait_recv()
            for place in range(4):
                multiply(behind * 4 + place, 1)

        return 0

    lax.fori_loop(1, last + 2, on_step, 0)

    part = half // plane
    width = KT_DEV * 2
    spot_in_plane = line * 2 + lo
    for i in range(plane):
        for n in range(width):
            parts[i, n] = acc[i * part : (i + 1) * part, n * TILE : (n + 1) * TILE].astype(
                parts.dtype
            )

    def out_copy(step):
        target = (spot_in_plane + step) % plane
        return pltpu.make_async_remote_copy(
            src_ref=parts.at[target], dst_ref=natural.at[spot_in_plane],
            send_sem=out_send.at[step - 1], recv_sem=out_recv.at[step - 1],
            device_id={"vcol": (target // 2) * 4 + hi * 2 + target % 2}, device_id_type=MESH,
        )

    def back_copy(step):
        target = (me + step) % ranks
        return pltpu.make_async_remote_copy(
            src_ref=slots.at[target], dst_ref=landed.at[me],
            send_sem=back_send.at[step - 1], recv_sem=back_recv.at[step - 1],
            device_id={"vcol": target}, device_id_type=MESH,
        )

    def each(count, action):
        def body(step, _):
            action(step)
            return 0

        lax.fori_loop(1, count, body, 0)

    each(plane, lambda step: out_copy(step).start())
    own_out = pltpu.make_async_copy(
        parts.at[spot_in_plane], natural.at[spot_in_plane], local_sem.at[2]
    )
    own_out.start()
    own_out.wait()
    each(plane, lambda step: out_copy(step).wait_recv())
    for j in range(ranks):
        for n in range(KT_DEV):
            tile = owner[KT_DEV * j + n]
            chip, odd = tile // KT_DEV, tile % KT_DEV
            row, col = (chip % 4) // 2, chip % 2
            slots[j, n] = natural[(chip // 4) * 2 + col, ((row + hi) % 2) * KT_DEV + odd]
    each(ranks, lambda step: back_copy(step).start())
    own_back = pltpu.make_async_copy(slots.at[me], landed.at[me], local_sem.at[3])
    own_back.start()
    own_back.wait()

    first_copies(wait_send)
    for band in (0, 1):
        forward(partner, band, jnp.int32(0), wait_send)

    def drain(e, _):
        @pl.when((e > 0) & inside(e))
        def _():
            for h in range(2):
                for band in (0, 1):
                    forward((line + offset(e)) * 4 + h * 2 + lo, band, e, wait_send)

        def close(chunk):
            far_copy(chunk).wait_send()
            for step in range(1, pairs):
                pass_copy(chunk, step, core).wait_send()

        on_line(e, close)
        return 0

    lax.fori_loop(0, last, drain, 0)
    for step in range(1, pairs):
        panel_copy(step).wait_send()
    each(plane, lambda step: out_copy(step).wait_send())
    each(ranks, lambda step: back_copy(step).wait_recv())
    for j in range(ranks):
        base = ((j % 4) // 2) * half + ((j // 4) * 2 + j % 2) * part
        for n in range(KT_DEV):
            out[base : base + part, n * TILE : (n + 1) * TILE] = landed[j, n].astype(out.dtype)
    each(ranks, lambda step: back_copy(step).wait_send())


def ladder(ranks, pairs, amplitudes, tile_owner, integrals, screening):
    rows, width = amplitudes.shape
    tiles = integrals.shape[0] // TILE
    half, plane = rows // 2, ranks // 2
    chunks = KT_DEV * ranks // pairs
    vmem, smem = pl.BlockSpec(memory_space=pltpu.VMEM), pl.BlockSpec(memory_space=pltpu.SMEM)
    hbm = pl.BlockSpec(memory_space=pl.ANY)
    part = half // plane
    dma = pltpu.SemaphoreType.DMA
    return pl.pallas_call(
        functools.partial(ladder_kernel, ranks, pairs),
        out_shape=jax.ShapeDtypeStruct((rows, width), jnp.float32),
        in_specs=[smem, smem, hbm, hbm],
        out_specs=vmem,
        scratch_shapes=[
            pltpu.VMEM((ranks, half, width), jnp.bfloat16),
            pltpu.VMEM((tiles * pairs, TILE, width), jnp.bfloat16),
            pltpu.VMEM((chunks, TILE, width), jnp.bfloat16),
            pltpu.VMEM((KT_DEV * ranks, TILE, width), jnp.bfloat16),
            pltpu.VMEM((KT_DEV, half, width), jnp.bfloat16),
            pltpu.VMEM((half, 2 * width), jnp.float32),
            pltpu.VMEM((plane, 2 * KT_DEV, part, TILE), jnp.bfloat16),
            pltpu.VMEM((plane, 2 * KT_DEV, part, TILE), jnp.bfloat16),
            pltpu.VMEM((ranks, KT_DEV, part, TILE), jnp.bfloat16),
            pltpu.VMEM((ranks, KT_DEV, part, TILE), jnp.bfloat16),
            dma((4,)),
            dma((2, 4, ranks)),
            dma((2, ranks)),
            dma((pairs - 1,)),
            dma((pairs - 1,)),
            dma((chunks,)),
            dma((chunks,)),
            dma((pairs - 1, chunks)),
            dma((pairs - 1, chunks)),
            dma((plane - 1,)),
            dma((plane - 1,)),
            dma((ranks - 1,)),
            dma((ranks - 1,)),
        ],
        compiler_params=pltpu.CompilerParams(
            collective_id=0, has_side_effects=True, vmem_limit_bytes=62 * 1024 * 1024
        ),
    )(tile_owner, screening, amplitudes, integrals.reshape(tiles, TILE, width))


def local(ranks, pairs, amplitudes, tile_owner, integrals, screening, occ_energy, virt_energy):
    tile_count = tile_owner.shape[0]
    width = KT_DEV * TILE
    column = lax.axis_index("vcol")
    owned_tiles = lax.dynamic_slice_in_dim(tile_owner, column * KT_DEV, KT_DEV, 0)
    ladder_owned = ladder(ranks, pairs, amplitudes, tile_owner, integrals, screening)
    virt_owned = jnp.dot(
        one_hot(owned_tiles, tile_count),
        virt_energy.reshape(tile_count, TILE),
        precision=lax.Precision.HIGHEST,
    ).reshape(width)
    residual = ladder_owned + (virt_owned[None, :] - occ_energy[:, None]) * amplitudes.astype(
        jnp.float32
    )
    return residual.astype(jnp.bfloat16)


def solution(mesh):
    return jax.shard_map(
        functools.partial(local, mesh.shape["vcol"], mesh.shape["pair"]),
        mesh=mesh,
        in_specs=(P("pair", "vcol"), P(), P("pair", "vcol"), P("pair", None, None), P("pair"), P()),
        out_specs=P("pair", "vcol"),
        check_vma=False,
    )
```

```python
import functools

import jax
import jax.numpy as jnp
from jax import lax
from jax.experimental import pallas as pl
from jax.experimental.pallas import tpu as pltpu
from jax.sharding import PartitionSpec as P

TILE = 128
PBLK = 64
KT_DEV = 2
MESH = pl.DeviceIdType.MESH
UP, DOWN, BESIDE, PARTNER = 0, 1, 2, 3


def band_edges(half):
    cut = (half // PBLK * 3 // 5) * PBLK
    return ((0, cut), (cut, half))


def ladder_kernel(
    ranks, pairs, amps, owner_in, ints, screen_in, occ_in, virt_in, out,
    owner, screen, occ, virt, mine, base, gath, panel, stage, far, lhs, acc,
    parts0, parts1, natural0, natural1, slots0, slots1, landed0, landed1,
    local_sem, send_sem, recv_sem, pair_send, pair_recv, far_send, far_recv, pass_send, pass_recv,
    out_send, out_recv, back_send, back_recv,
):
    length = ranks // 4
    plane = ranks // 2
    groups = pairs // 2
    me = lax.axis_index("vcol")
    core = lax.axis_index("pair")
    line, spot = me // 4, me % 4
    hi, lo = spot // 2, spot % 2
    beside = line * 4 + hi * 2 + (1 - lo)
    partner = line * 4 + (1 - hi) * 2 + lo
    has_up, has_down = line < length - 1, line > 0
    half = gath.shape[1]
    blocks = half // PBLK
    tiles = ints.shape[0]
    bands = band_edges(half)

    def load(index, source, target):
        return pltpu.make_async_copy(source, target, local_sem.at[index])

    own_ints = load(0, ints, panel.at[pl.ds(core * tiles, tiles)])
    own_amps = load(1, amps.at[pl.ds(hi * half, half)], gath.at[me])
    get_owner = load(2, owner_in, owner)
    get_screen = load(3, screen_in.at[pl.ds(hi * blocks, blocks)], screen)
    get_occ = load(4, occ_in, occ)
    get_virt = load(5, virt_in, virt)
    get_mine = load(6, amps, mine)
    loads = (get_owner, own_ints, get_screen, own_amps, get_occ, get_virt, get_mine)

    barrier = pltpu.get_barrier_semaphore()

    def greet(target):
        pl.semaphore_signal(barrier, inc=1, device_id={"vcol": target}, device_id_type=MESH)

    greet(beside)
    greet(partner)
    pl.when(has_up)(lambda: greet(me + 4))
    pl.when(has_down)(lambda: greet(me - 4))
    for step in range(1, pairs):
        pl.semaphore_signal(
            barrier, inc=1, device_id={"pair": (core + step) % pairs}, device_id_type=MESH
        )
    for copy in loads:
        copy.start()
    pl.semaphore_wait(
        barrier, pairs + 1 + has_up.astype(jnp.int32) + has_down.astype(jnp.int32)
    )

    def first_copy(band, way, target):
        low, high = bands[band]
        start_row = (1 - hi) * half if way == PARTNER else hi * half
        return pltpu.make_async_remote_copy(
            src_ref=amps.at[pl.ds(start_row + low, high - low)],
            dst_ref=gath.at[me, pl.ds(low, high - low)],
            send_sem=send_sem.at[band, way, me], recv_sem=recv_sem.at[band, me],
            device_id={"vcol": target}, device_id_type=MESH,
        )

    def relay(source, band, way, target):
        low, high = bands[band]
        place = gath.at[source, pl.ds(low, high - low)]
        return pltpu.make_async_remote_copy(
            src_ref=place, dst_ref=place,
            send_sem=send_sem.at[band, way, source], recv_sem=recv_sem.at[band, source],
            device_id={"vcol": target}, device_id_type=MESH,
        )

    def panel_copy(step):
        return pltpu.make_async_remote_copy(
            src_ref=ints, dst_ref=panel.at[pl.ds(core * tiles, tiles)],
            send_sem=pair_send.at[step - 1], recv_sem=pair_recv.at[step - 1],
            device_id={"pair": (core + step) % pairs}, device_id_type=MESH,
        )

    def far_copy(source):
        return pltpu.make_async_remote_copy(
            src_ref=stage.at[source], dst_ref=far.at[KT_DEV * source + core % 2],
            send_sem=far_send.at[source], recv_sem=far_recv.at[source],
            device_id={"vcol": partner}, device_id_type=MESH,
        )

    def pass_copy(source, step, holder):
        slot = KT_DEV * source + holder % 2
        return pltpu.make_async_remote_copy(
            src_ref=far.at[slot], dst_ref=far.at[slot],
            send_sem=pass_send.at[step - 1, slot], recv_sem=pass_recv.at[slot],
            device_id={"pair": (core + step) % pairs}, device_id_type=MESH,
        )

    def if_holder(source, holder, action):
        if groups == 1:
            action()
        else:
            pl.when(source % groups == holder // 2)(action)

    def start(copy):
        copy.start()

    def wait_send(copy):
        copy.wait_send()

    def inside(at):
        return (at >= 0) & (at < length)

    def skipped(at):
        low = jnp.where(at % 2 == 0, at + 2, at - 1)
        high = jnp.where(at % 2 == 0, at + 1, at - 2)
        return jnp.where(at < length // 2, low, high)

    mate = line + 1 - 2 * (line % 2)
    skip, mate_skip = skipped(line), skipped(mate)

    def on_level(level, action):
        odd = level % 2
        h = hi + odd - 2 * hi * odd
        for x in (0, 1):
            d = level // 2 - x
            for away in (-1, 1):
                at = line + away * d
                valid = (d > 0 if away < 0 else d >= 0) & inside(at)
                pl.when(valid)(functools.partial(action, x, at, h, odd))

    def unit(at, h, x):
        return at * 4 + h * 2 + (1 - lo if x else lo)

    def onward(x, at, h, odd, band, action):
        source = unit(at, h, x)
        if x == 0:
            pl.when((at <= line) & has_up)(lambda: action(relay(source, band, UP, me + 4)))
            pl.when((at >= line) & has_down)(lambda: action(relay(source, band, DOWN, me - 4)))
            pl.when((at != skip) | (odd == 0))(
                lambda: action(relay(source, band, BESIDE, beside))
            )
        else:
            wanted = (at == mate_skip) & (odd == 1)
            pl.when(wanted & (mate > line))(lambda: action(relay(source, band, UP, me + 4)))
            pl.when(wanted & (mate < line))(lambda: action(relay(source, band, DOWN, me - 4)))

    def first_copies(action):
        for band in (0, 1):
            action(first_copy(band, PARTNER, partner))
            pl.when(has_up)(lambda: action(first_copy(band, UP, me + 4)))
            pl.when(has_down)(lambda: action(first_copy(band, DOWN, me - 4)))
            action(first_copy(band, BESIDE, beside))

    def multiply(source, side, first, stop):
        tile_pair = (owner[KT_DEV * source], owner[KT_DEV * source + 1])
        home = partner if side else me
        rows = slice(first * PBLK, stop * PBLK)
        for slot, tile in enumerate(tile_pair):
            columns = slice(slot * TILE, (slot + 1) * TILE)
            for block in range(first, stop):
                part = slice(block * PBLK, (block + 1) * PBLK)
                value = gath[source, part, columns]
                for n in range(KT_DEV):
                    mark = screen[block, tile, KT_DEV * home + n].astype(jnp.float32)
                    lhs[n, part, columns] = value * jnp.full(value.shape, mark, jnp.float32).astype(
                        value.dtype
                    )
        if side:
            right = jnp.concatenate([far[KT_DEV * source], far[KT_DEV * source + 1]], axis=0)
        else:
            right = jnp.concatenate([panel[tile] for tile in tile_pair], axis=0)
        for n in range(KT_DEV):
            columns = slice(n * TILE, (n + 1) * TILE)
            place = slice((KT_DEV * side + n) * TILE, (KT_DEV * side + n + 1) * TILE)
            acc[rows, place] += jnp.dot(
                lhs[n, rows], right[:, columns], preferred_element_type=jnp.float32
            )

    first_copies(start)
    for step in range(1, pairs):
        panel_copy(step).start()
    acc[...] = jnp.zeros_like(acc)
    get_owner.wait()
    own_ints.wait()
    for step in range(1, pairs):
        panel_copy(step).wait_recv()

    def fill(source, _):
        if_holder(
            source, core,
            lambda: stage.__setitem__(source, panel[owner[KT_DEV * source + core % 2]]),
        )
        return 0

    def to_partner(action):
        def body(level, _):
            def send(x, at, h, odd):
                source = unit(at, 1 - h, x)
                if_holder(source, core, lambda: action(far_copy(source)))

            on_level(level, send)
            return 0

        lax.fori_loop(0, 2 * length + 2, body, 0)

    lax.fori_loop(0, ranks, fill, 0)
    to_partner(start)

    def pass_on(source):
        def go():
            far_copy(source).wait_recv()
            for step in range(1, pairs):
                pass_copy(source, step, core).start()

        if_holder(source, core, go)

    def passed(source):
        for step in range(1, pairs):
            holder = (core + step) % pairs
            if_holder(
                source, holder, lambda: pass_copy(source, step, holder).wait_recv()
            )

    def arrived(source, band):
        relay(source, band, BESIDE, beside).wait_recv()

    def far_whole(source):
        passed(source)
        multiply(source, 1, 0, blocks)

    get_screen.wait()
    own_amps.wait()
    multiply(me, 0, 0, blocks)

    def on_unit(action):
        return lambda x, at, h, odd: action(unit(at, h, x))

    def run_level(level, _):
        for band in (0, 1):

            def take(x, at, h, odd):
                arrived(unit(at, h, x), band)
                onward(x, at, h, odd, band, start)

            on_level(level, take)
        on_level(level - 1, on_unit(pass_on))
        on_level(level, on_unit(lambda source: multiply(source, 0, 0, blocks)))
        on_level(level - 1, on_unit(far_whole))
        return 0

    final = 2 * length + 1

    lax.fori_loop(1, final, run_level, 0)
    on_level(final - 1, on_unit(pass_on))
    on_level(final, on_unit(pass_on))
    on_level(final - 1, on_unit(far_whole))
    on_level(final, on_unit(passed))

    spot_in_plane = line * 2 + lo
    parts, natural = (parts0, parts1), (natural0, natural1)
    slots, landed = (slots0, slots1), (landed0, landed1)

    def out_copy(band, step):
        target = (spot_in_plane + step) % plane
        return pltpu.make_async_remote_copy(
            src_ref=parts[band].at[target], dst_ref=natural[band].at[spot_in_plane],
            send_sem=out_send.at[band, step - 1], recv_sem=out_recv.at[band, step - 1],
            device_id={"vcol": (target // 2) * 4 + hi * 2 + target % 2}, device_id_type=MESH,
        )

    def back_copy(band, step):
        target = (me + step) % ranks
        return pltpu.make_async_remote_copy(
            src_ref=slots[band].at[target], dst_ref=landed[band].at[me],
            send_sem=back_send.at[band, step - 1], recv_sem=back_recv.at[band, step - 1],
            device_id={"vcol": target}, device_id_type=MESH,
        )

    def each(count, action):
        def body(step, _):
            action(step)
            return 0

        lax.fori_loop(1, count, body, 0)

    for band in (0, 1):
        low, high = bands[band]

        def finish(source):
            arrived(source, band)
            for side in (0, 1):
                multiply(source, side, low // PBLK, high // PBLK)

        on_level(final, on_unit(finish))
        part = (high - low) // plane
        for i in range(plane):
            for n in range(2 * KT_DEV):
                parts[band][i, n] = acc[
                    low + i * part : low + (i + 1) * part, n * TILE : (n + 1) * TILE
                ].astype(jnp.bfloat16)
        each(plane, lambda step: out_copy(band, step).start())
        natural[band][spot_in_plane] = parts[band][spot_in_plane]

    get_occ.wait()
    get_virt.wait()
    get_mine.wait()
    rows = mine.shape[0]
    eye = lax.broadcasted_iota(jnp.int32, (TILE, TILE), 0) == lax.broadcasted_iota(
        jnp.int32, (TILE, TILE), 1
    )
    for g in range(rows // TILE):
        part = slice(g * TILE, (g + 1) * TILE)
        spread = jnp.broadcast_to(occ[g : g + 1, :], (TILE, TILE))
        column = jnp.sum(jnp.where(eye, spread, 0.0), axis=1, keepdims=True)
        for n in range(KT_DEV):
            columns = slice(n * TILE, (n + 1) * TILE)
            level = virt[pl.ds(owner[KT_DEV * me + n], 1), :]
            base[part, columns] = (level - column) * mine[part, columns].astype(jnp.float32)

    for band in (0, 1):
        each(plane, lambda step: out_copy(band, step).wait_recv())
        for j in range(ranks):
            for n in range(KT_DEV):
                tile = owner[KT_DEV * j + n]
                home, odd = tile // KT_DEV, tile % KT_DEV
                row, col = (home % 4) // 2, home % 2
                slots[band][j, n] = natural[band][
                    (home // 4) * 2 + col, ((row + hi) % 2) * KT_DEV + odd
                ]
        each(ranks, lambda step: back_copy(band, step).start())
        landed[band][me] = slots[band][me]

    first_copies(wait_send)

    def drain(level, _):
        for band in (0, 1):
            on_level(
                level, lambda x, at, h, odd: onward(x, at, h, odd, band, wait_send)
            )
        return 0

    lax.fori_loop(1, final + 1, drain, 0)
    to_partner(wait_send)

    def close(source, _):
        def go():
            for step in range(1, pairs):
                pass_copy(source, step, core).wait_send()

        if_holder(source, core, go)
        return 0

    lax.fori_loop(0, ranks, close, 0)
    for step in range(1, pairs):
        panel_copy(step).wait_send()
    for band in (0, 1):
        each(plane, lambda step: out_copy(band, step).wait_send())

    for band in (0, 1):
        low, high = bands[band]
        part = (high - low) // plane
        each(ranks, lambda step: back_copy(band, step).wait_recv())
        for j in range(ranks):
            at = ((j % 4) // 2) * half + low + ((j // 4) * 2 + j % 2) * part
            for n in range(KT_DEV):
                columns = slice(n * TILE, (n + 1) * TILE)
                out[at : at + part, columns] = (
                    landed[band][j, n].astype(jnp.float32) + base[at : at + part, columns]
                ).astype(out.dtype)
    for band in (0, 1):
        each(ranks, lambda step: back_copy(band, step).wait_send())


def local(ranks, pairs, amplitudes, tile_owner, integrals, screening, occ_energy, virt_energy):
    rows, width = amplitudes.shape
    tiles = integrals.shape[0] // TILE
    count = tile_owner.shape[0]
    half, plane = rows // 2, ranks // 2
    blocks = half // PBLK
    hbm = pl.BlockSpec(memory_space=pl.ANY)
    dma = pltpu.SemaphoreType.DMA
    sizes = [(high - low) // plane for low, high in band_edges(half)]

    def exchange(lead, tiles_each):
        return [pltpu.VMEM((lead, tiles_each, size, TILE), jnp.bfloat16) for size in sizes]

    return pl.pallas_call(
        functools.partial(ladder_kernel, ranks, pairs),
        out_shape=jax.ShapeDtypeStruct((rows, width), jnp.bfloat16),
        in_specs=[hbm] * 6,
        out_specs=pl.BlockSpec(memory_space=pltpu.VMEM),
        scratch_shapes=[
            pltpu.SMEM((count,), jnp.int32),
            pltpu.SMEM((blocks, count, count), jnp.int32),
            pltpu.VMEM((rows // TILE, TILE), jnp.float32),
            pltpu.VMEM((count, TILE), jnp.float32),
            pltpu.VMEM((rows, width), jnp.bfloat16),
            pltpu.VMEM((rows, width), jnp.float32),
            pltpu.VMEM((ranks, half, width), jnp.bfloat16),
            pltpu.VMEM((tiles * pairs, TILE, width), jnp.bfloat16),
            pltpu.VMEM((ranks, TILE, width), jnp.bfloat16),
            pltpu.VMEM((KT_DEV * ranks, TILE, width), jnp.bfloat16),
            pltpu.VMEM((KT_DEV, half, width), jnp.bfloat16),
            pltpu.VMEM((half, 2 * width), jnp.float32),
            *exchange(plane, 2 * KT_DEV),
            *exchange(plane, 2 * KT_DEV),
            *exchange(ranks, KT_DEV),
            *exchange(ranks, KT_DEV),
            dma((7,)),
            dma((2, 4, ranks)),
            dma((2, ranks)),
            dma((pairs - 1,)),
            dma((pairs - 1,)),
            dma((ranks,)),
            dma((ranks,)),
            dma((pairs - 1, KT_DEV * ranks)),
            dma((KT_DEV * ranks,)),
            dma((2, plane - 1)),
            dma((2, plane - 1)),
            dma((2, ranks - 1)),
            dma((2, ranks - 1)),
        ],
        compiler_params=pltpu.CompilerParams(
            collective_id=0, has_side_effects=True, vmem_limit_bytes=62 * 1024 * 1024
        ),
    )(
        amplitudes,
        tile_owner,
        integrals.reshape(tiles, TILE, width),
        screening,
        occ_energy.reshape(rows // TILE, TILE),
        virt_energy.reshape(count, TILE),
    )


def solution(mesh):
    return jax.shard_map(
        functools.partial(local, mesh.shape["vcol"], mesh.shape["pair"]),
        mesh=mesh,
        in_specs=(P("pair", "vcol"), P(), P("pair", "vcol"), P("pair", None, None), P("pair"), P()),
        out_specs=P("pair", "vcol"),
        check_vma=False,
    )
```

```python
import functools

import jax
import jax.numpy as jnp
from jax import lax
from jax.experimental import pallas as pl
from jax.experimental.pallas import tpu as pltpu
from jax.sharding import PartitionSpec as P

TILE = 128
PBLK = 64
KT_DEV = 2
MESH = pl.DeviceIdType.MESH
UP, DOWN, BESIDE, PARTNER = 0, 1, 2, 3


def band_edges(half):
    cut = (half // PBLK * 3 // 5) * PBLK
    return ((0, cut), (cut, half))


def ladder_kernel(
    ranks, pairs, amps, owner_in, ints, screen_in, occ_in, virt_in, out,
    owner, place, screen, occ, virt, mine, base, gath, panel, stage, far, lhs, acc,
    parts0, parts1, natural0, natural1, slots0, slots1, landed0, landed1,
    local_sem, send_sem, recv_sem, pair_send, pair_recv, far_send, far_recv, pass_send, pass_recv,
    out_send, out_recv, back_send, back_recv,
):
    length = ranks // 4
    plane = ranks // 2
    groups = pairs // 2
    me = lax.axis_index("vcol")
    core = lax.axis_index("pair")
    line, spot = me // 4, me % 4
    hi, lo = spot // 2, spot % 2
    beside = line * 4 + hi * 2 + (1 - lo)
    partner = line * 4 + (1 - hi) * 2 + lo
    has_up, has_down = line < length - 1, line > 0
    half = gath.shape[1]
    blocks = half // PBLK
    tiles = ints.shape[0]
    bands = band_edges(half)

    def load(index, source, target):
        return pltpu.make_async_copy(source, target, local_sem.at[index])

    own_ints = load(0, ints, panel.at[pl.ds(core * tiles, tiles)])
    own_amps = load(1, amps.at[pl.ds(hi * half, half)], gath.at[me])
    get_owner = load(2, owner_in, owner)
    get_screen = load(3, screen_in.at[pl.ds(hi * blocks, blocks)], screen)
    get_occ = load(4, occ_in, occ)
    get_virt = load(5, virt_in, virt)
    get_mine = load(6, amps, mine)
    loads = (get_owner, own_ints, get_screen, own_amps, get_occ, get_virt, get_mine)

    barrier = pltpu.get_barrier_semaphore()

    def greet(target):
        pl.semaphore_signal(barrier, inc=1, device_id={"vcol": target}, device_id_type=MESH)

    greet(beside)
    greet(partner)
    pl.when(has_up)(lambda: greet(me + 4))
    pl.when(has_down)(lambda: greet(me - 4))
    for step in range(1, pairs):
        pl.semaphore_signal(
            barrier, inc=1, device_id={"pair": (core + step) % pairs}, device_id_type=MESH
        )
    for copy in loads:
        copy.start()
    pl.semaphore_wait(
        barrier, pairs + 1 + has_up.astype(jnp.int32) + has_down.astype(jnp.int32)
    )

    def first_copy(band, way, target):
        low, high = bands[band]
        start_row = (1 - hi) * half if way == PARTNER else hi * half
        return pltpu.make_async_remote_copy(
            src_ref=amps.at[pl.ds(start_row + low, high - low)],
            dst_ref=gath.at[me, pl.ds(low, high - low)],
            send_sem=send_sem.at[band, way, me], recv_sem=recv_sem.at[band, me],
            device_id={"vcol": target}, device_id_type=MESH,
        )

    def relay(source, band, way, target):
        low, high = bands[band]
        place = gath.at[source, pl.ds(low, high - low)]
        return pltpu.make_async_remote_copy(
            src_ref=place, dst_ref=place,
            send_sem=send_sem.at[band, way, source], recv_sem=recv_sem.at[band, source],
            device_id={"vcol": target}, device_id_type=MESH,
        )

    def panel_copy(step):
        return pltpu.make_async_remote_copy(
            src_ref=ints, dst_ref=panel.at[pl.ds(core * tiles, tiles)],
            send_sem=pair_send.at[step - 1], recv_sem=pair_recv.at[step - 1],
            device_id={"pair": (core + step) % pairs}, device_id_type=MESH,
        )

    def far_copy(source):
        return pltpu.make_async_remote_copy(
            src_ref=stage.at[source], dst_ref=far.at[KT_DEV * source + core % 2],
            send_sem=far_send.at[source], recv_sem=far_recv.at[source],
            device_id={"vcol": partner}, device_id_type=MESH,
        )

    def pass_copy(source, step, holder):
        slot = KT_DEV * source + holder % 2
        return pltpu.make_async_remote_copy(
            src_ref=far.at[slot], dst_ref=far.at[slot],
            send_sem=pass_send.at[step - 1, slot], recv_sem=pass_recv.at[slot],
            device_id={"pair": (core + step) % pairs}, device_id_type=MESH,
        )

    def if_holder(source, holder, action):
        if groups == 1:
            action()
        else:
            pl.when(source % groups == holder // 2)(action)

    def start(copy):
        copy.start()

    def wait_send(copy):
        copy.wait_send()

    def inside(at):
        return (at >= 0) & (at < length)

    def skipped(at):
        low = jnp.where(at % 2 == 0, at + 2, at - 1)
        high = jnp.where(at % 2 == 0, at + 1, at - 2)
        return jnp.where(at < length // 2, low, high)

    mate = line + 1 - 2 * (line % 2)
    skip, mate_skip = skipped(line), skipped(mate)

    def on_level(level, action):
        odd = level % 2
        h = hi + odd - 2 * hi * odd
        for x in (0, 1):
            d = level // 2 - x
            for away in (-1, 1):
                at = line + away * d
                valid = (d > 0 if away < 0 else d >= 0) & inside(at)
                if x == 1:
                    valid = valid & ((at != skip) | (odd == 0))
                pl.when(valid)(functools.partial(action, x, at, h, odd))

    def unit(at, h, x):
        return at * 4 + h * 2 + (1 - lo if x else lo)

    def onward(x, at, h, odd, band, action):
        source = unit(at, h, x)
        if x == 0:
            pl.when((at <= line) & has_up)(lambda: action(relay(source, band, UP, me + 4)))
            pl.when((at >= line) & has_down)(lambda: action(relay(source, band, DOWN, me - 4)))
            pl.when((at != skip) | (odd == 0))(
                lambda: action(relay(source, band, BESIDE, beside))
            )
        else:
            wanted = (at == mate_skip) & (odd == 1)
            pl.when(wanted & (mate > line))(lambda: action(relay(source, band, UP, me + 4)))
            pl.when(wanted & (mate < line))(lambda: action(relay(source, band, DOWN, me - 4)))

    def first_copies(action):
        for band in (0, 1):
            action(first_copy(band, PARTNER, partner))
            pl.when(has_up)(lambda: action(first_copy(band, UP, me + 4)))
            pl.when(has_down)(lambda: action(first_copy(band, DOWN, me - 4)))
            action(first_copy(band, BESIDE, beside))

    def multiply(source, side, first, stop):
        tile_pair = (owner[KT_DEV * source], owner[KT_DEV * source + 1])
        home = partner if side else me
        rows = slice(first * PBLK, stop * PBLK)
        for slot, tile in enumerate(tile_pair):
            columns = slice(slot * TILE, (slot + 1) * TILE)
            for block in range(first, stop):
                part = slice(block * PBLK, (block + 1) * PBLK)
                value = gath[source, part, columns]
                for n in range(KT_DEV):
                    mark = screen[block, tile, KT_DEV * home + n].astype(jnp.float32)
                    lhs[n, part, columns] = value * jnp.full(value.shape, mark, jnp.float32).astype(
                        value.dtype
                    )
        if side:
            right = jnp.concatenate([far[KT_DEV * source], far[KT_DEV * source + 1]], axis=0)
        else:
            right = jnp.concatenate([panel[tile] for tile in tile_pair], axis=0)
        for n in range(KT_DEV):
            columns = slice(n * TILE, (n + 1) * TILE)
            place = slice((KT_DEV * side + n) * TILE, (KT_DEV * side + n + 1) * TILE)
            acc[rows, place] += jnp.dot(
                lhs[n, rows], right[:, columns], preferred_element_type=jnp.float32
            )

    first_copies(start)
    for step in range(1, pairs):
        panel_copy(step).start()
    acc[...] = jnp.zeros_like(acc)
    get_owner.wait()
    own_ints.wait()
    for step in range(1, pairs):
        panel_copy(step).wait_recv()

    def fill(source, _):
        if_holder(
            source, core,
            lambda: stage.__setitem__(source, panel[owner[KT_DEV * source + core % 2]]),
        )
        return 0

    def to_partner(action):
        def body(level, _):
            def send(x, at, h, odd):
                source = unit(at, 1 - h, x)
                if_holder(source, core, lambda: action(far_copy(source)))

            on_level(level, send)
            return 0

        lax.fori_loop(0, 2 * length + 2, body, 0)
        source = unit(skip, hi, 1)
        if_holder(source, core, lambda: action(far_copy(source)))

    lax.fori_loop(0, ranks, fill, 0)
    to_partner(start)

    def pass_on(source):
        def go():
            far_copy(source).wait_recv()
            for step in range(1, pairs):
                pass_copy(source, step, core).start()

        if_holder(source, core, go)

    def passed(source):
        for step in range(1, pairs):
            holder = (core + step) % pairs
            if_holder(
                source, holder, lambda: pass_copy(source, step, holder).wait_recv()
            )

    def arrived(source, band):
        relay(source, band, BESIDE, beside).wait_recv()

    def far_whole(source):
        passed(source)
        multiply(source, 1, 0, blocks)

    def find(slot, _):
        tile = owner[slot]
        row, col = (tile >> 2) & 1, (tile >> 1) & 1
        place[slot] = (tile & -8) | (col << 2) | ((row ^ hi) << 1) | (tile & 1)
        return 0

    lax.fori_loop(0, KT_DEV * ranks, find, 0)
    get_screen.wait()
    own_amps.wait()
    multiply(me, 0, 0, blocks)

    def on_unit(action):
        return lambda x, at, h, odd: action(unit(at, h, x))

    def relay_level(level):
        for band in (0, 1):

            def take(x, at, h, odd):
                arrived(unit(at, h, x), band)
                onward(x, at, h, odd, band, start)

            on_level(level, take)

    def near_level(level):
        on_level(level, on_unit(lambda source: multiply(source, 0, 0, blocks)))

    def early_level(level, _):
        relay_level(level)
        on_level(level - 1, on_unit(pass_on))
        near_level(level)
        on_level(level - 1, on_unit(far_whole))
        return 0

    def late_level(level, _):
        on_level(level, on_unit(pass_on))
        relay_level(level)
        near_level(level)
        on_level(level - 1, on_unit(far_whole))
        return 0

    final = 2 * length + 1
    skipped_unit = unit(skip, 1 - hi, 1)

    lax.fori_loop(1, final - 2, early_level, 0)
    on_level(final - 3, on_unit(pass_on))
    lax.fori_loop(final - 2, final, late_level, 0)
    on_level(final, on_unit(pass_on))
    pass_on(skipped_unit)
    on_level(final - 1, on_unit(far_whole))
    on_level(final, on_unit(passed))
    passed(skipped_unit)

    spot_in_plane = line * 2 + lo
    parts, natural = (parts0, parts1), (natural0, natural1)
    slots, landed = (slots0, slots1), (landed0, landed1)

    def nearest(k, here, count):
        wide = count // length
        d = k // wide
        low = jnp.minimum(line, length - 1 - line)
        paired = line + ((d + 1) // 2) * (1 - 2 * (d % 2))
        single = jnp.where(line < length // 2, d, length - 1 - d)
        return jnp.where(d <= 2 * low, paired, single) * wide + (here + k) % wide

    def out_copy(band, source, target):
        return pltpu.make_async_remote_copy(
            src_ref=parts[band].at[target], dst_ref=natural[band].at[pl.ds(source * 4, 4)],
            send_sem=out_send.at[band, target], recv_sem=out_recv.at[band, source],
            device_id={"vcol": (target // 2) * 4 + hi * 2 + target % 2}, device_id_type=MESH,
        )

    def back_copy(band, source, target):
        return pltpu.make_async_remote_copy(
            src_ref=slots[band].at[target], dst_ref=landed[band].at[source],
            send_sem=back_send.at[band, target], recv_sem=back_recv.at[band, source],
            device_id={"vcol": target}, device_id_type=MESH,
        )

    def send_each(copy, band, here, count, action):
        def body(step, _):
            action(copy(band, here, nearest(count - step, here, count)))
            return 0

        lax.fori_loop(1, count, body, 0)

    def take_each(copy, band, here, count):
        def body(step, _):
            copy(band, (here + step) % count, here).wait_recv()
            return 0

        lax.fori_loop(1, count, body, 0)

    for band in (0, 1):
        low, high = bands[band]

        def finish(source):
            arrived(source, band)
            for side in (0, 1):
                multiply(source, side, low // PBLK, high // PBLK)

        on_level(final, on_unit(finish))
        finish(skipped_unit)
        part = (high - low) // plane
        for i in range(plane):
            for n in range(2 * KT_DEV):
                parts[band][i, n] = acc[
                    low + i * part : low + (i + 1) * part, n * TILE : (n + 1) * TILE
                ].astype(jnp.bfloat16)
        send_each(out_copy, band, spot_in_plane, plane, start)
        natural[band][pl.ds(spot_in_plane * 4, 4)] = parts[band][spot_in_plane]

    get_occ.wait()
    get_virt.wait()
    get_mine.wait()
    rows = mine.shape[0]
    eye = lax.broadcasted_iota(jnp.int32, (TILE, TILE), 0) == lax.broadcasted_iota(
        jnp.int32, (TILE, TILE), 1
    )
    for g in range(rows // TILE):
        part = slice(g * TILE, (g + 1) * TILE)
        spread = jnp.broadcast_to(occ[g : g + 1, :], (TILE, TILE))
        column = jnp.sum(jnp.where(eye, spread, 0.0), axis=1, keepdims=True)
        for n in range(KT_DEV):
            columns = slice(n * TILE, (n + 1) * TILE)
            level = virt[pl.ds(owner[KT_DEV * me + n], 1), :]
            base[part, columns] = (level - column) * mine[part, columns].astype(jnp.float32)

    for band in (0, 1):
        take_each(out_copy, band, spot_in_plane, plane)
        for j in range(ranks):
            for n in range(KT_DEV):
                slots[band][j, n] = natural[band][place[KT_DEV * j + n]]
        send_each(back_copy, band, me, ranks, start)
        landed[band][me] = slots[band][me]

    first_copies(wait_send)

    def drain(level, _):
        for band in (0, 1):
            on_level(
                level, lambda x, at, h, odd: onward(x, at, h, odd, band, wait_send)
            )
        return 0

    lax.fori_loop(1, final + 1, drain, 0)
    to_partner(wait_send)

    def close(source, _):
        def go():
            for step in range(1, pairs):
                pass_copy(source, step, core).wait_send()

        if_holder(source, core, go)
        return 0

    lax.fori_loop(0, ranks, close, 0)
    for step in range(1, pairs):
        panel_copy(step).wait_send()
    for band in (0, 1):
        send_each(out_copy, band, spot_in_plane, plane, wait_send)

    for band in (0, 1):
        low, high = bands[band]
        part = (high - low) // plane
        take_each(back_copy, band, me, ranks)
        for j in range(ranks):
            at = ((j % 4) // 2) * half + low + ((j // 4) * 2 + j % 2) * part
            for n in range(KT_DEV):
                columns = slice(n * TILE, (n + 1) * TILE)
                out[at : at + part, columns] = (
                    landed[band][j, n].astype(jnp.float32) + base[at : at + part, columns]
                ).astype(out.dtype)
    for band in (0, 1):
        send_each(back_copy, band, me, ranks, wait_send)


def local(ranks, pairs, amplitudes, tile_owner, integrals, screening, occ_energy, virt_energy):
    rows, width = amplitudes.shape
    tiles = integrals.shape[0] // TILE
    count = tile_owner.shape[0]
    half, plane = rows // 2, ranks // 2
    blocks = half // PBLK
    hbm = pl.BlockSpec(memory_space=pl.ANY)
    dma = pltpu.SemaphoreType.DMA
    sizes = [(high - low) // plane for low, high in band_edges(half)]

    def exchange(lead):
        return [pltpu.VMEM((*lead, size, TILE), jnp.bfloat16) for size in sizes]

    return pl.pallas_call(
        functools.partial(ladder_kernel, ranks, pairs),
        out_shape=pltpu.VMEM((rows, width), jnp.bfloat16),
        in_specs=[hbm] * 6,
        out_specs=pl.BlockSpec(memory_space=pltpu.VMEM),
        scratch_shapes=[
            pltpu.SMEM((count,), jnp.int32),
            pltpu.SMEM((count,), jnp.int32),
            pltpu.SMEM((blocks, count, count), jnp.int32),
            pltpu.VMEM((rows // TILE, TILE), jnp.float32),
            pltpu.VMEM((count, TILE), jnp.float32),
            pltpu.VMEM((rows, width), jnp.bfloat16),
            pltpu.VMEM((rows, width), jnp.float32),
            pltpu.VMEM((ranks, half, width), jnp.bfloat16),
            pltpu.VMEM((tiles * pairs, TILE, width), jnp.bfloat16),
            pltpu.VMEM((ranks, TILE, width), jnp.bfloat16),
            pltpu.VMEM((KT_DEV * ranks, TILE, width), jnp.bfloat16),
            pltpu.VMEM((KT_DEV, half, width), jnp.bfloat16),
            pltpu.VMEM((half, 2 * width), jnp.float32),
            *exchange((plane, 2 * KT_DEV)),
            *exchange((plane * 2 * KT_DEV,)),
            *exchange((ranks, KT_DEV)),
            *exchange((ranks, KT_DEV)),
            dma((7,)),
            dma((2, 4, ranks)),
            dma((2, ranks)),
            dma((pairs - 1,)),
            dma((pairs - 1,)),
            dma((ranks,)),
            dma((ranks,)),
            dma((pairs - 1, KT_DEV * ranks)),
            dma((KT_DEV * ranks,)),
            dma((2, plane)),
            dma((2, plane)),
            dma((2, ranks)),
            dma((2, ranks)),
        ],
        compiler_params=pltpu.CompilerParams(
            collective_id=0, has_side_effects=True, vmem_limit_bytes=62 * 1024 * 1024
        ),
    )(
        amplitudes,
        tile_owner,
        integrals.reshape(tiles, TILE, width),
        screening,
        occ_energy.reshape(rows // TILE, TILE),
        virt_energy.reshape(count, TILE),
    )


def solution(mesh):
    return jax.shard_map(
        functools.partial(local, mesh.shape["vcol"], mesh.shape["pair"]),
        mesh=mesh,
        in_specs=(P("pair", "vcol"), P(), P("pair", "vcol"), P("pair", None, None), P("pair"), P()),
        out_specs=P("pair", "vcol"),
        check_vma=False,
    )
```

```python
import functools

import jax
import jax.numpy as jnp
from jax import lax
from jax.experimental import pallas as pl
from jax.experimental.pallas import tpu as pltpu
from jax.sharding import PartitionSpec as P

TILE = 128
PBLK = 64
KT_DEV = 2
MESH = pl.DeviceIdType.MESH
UP, DOWN, BESIDE, PARTNER = 0, 1, 2, 3
SHARES = (2,)
BANDS = range(len(SHARES) + 1)


def band_edges(half):
    blocks = half // PBLK
    edges = [0, *(blocks * share // 5 * PBLK for share in SHARES), half]
    return tuple(zip(edges[:-1], edges[1:]))


def ladder_kernel(
    ranks, pairs, amps, owner_in, ints, screen_in, occ_in, virt_in, out,
    owner, place, screen, occ, virt, mine, base, gath, panel, stage, far, lhs, acc,
    parts, natural, slots, landed,
    local_sem, send_sem, recv_sem, pair_send, pair_recv, far_send, far_recv, pass_send, pass_recv,
    out_send, out_recv, back_send, back_recv,
):
    length = ranks // 4
    plane = ranks // 2
    groups = pairs // 2
    me = lax.axis_index("vcol")
    core = lax.axis_index("pair")
    line, spot = me // 4, me % 4
    hi, lo = spot // 2, spot % 2
    beside = line * 4 + hi * 2 + (1 - lo)
    partner = line * 4 + (1 - hi) * 2 + lo
    has_up, has_down = line < length - 1, line > 0
    half = gath.shape[1]
    blocks = half // PBLK
    tiles = ints.shape[0]
    bands = band_edges(half)

    def load(index, source, target):
        return pltpu.make_async_copy(source, target, local_sem.at[index])

    own_ints = load(0, ints, panel.at[pl.ds(core * tiles, tiles)])
    own_amps = load(1, amps.at[pl.ds(hi * half, half)], gath.at[me])
    get_owner = load(2, owner_in, owner)
    get_screen = load(3, screen_in.at[pl.ds(hi * blocks, blocks)], screen)
    get_occ = load(4, occ_in, occ)
    get_virt = load(5, virt_in, virt)
    get_mine = load(6, amps, mine)
    loads = (get_owner, own_ints, get_screen, own_amps, get_occ, get_virt, get_mine)

    barrier = pltpu.get_barrier_semaphore()

    def greet(target):
        pl.semaphore_signal(barrier, inc=1, device_id={"vcol": target}, device_id_type=MESH)

    greet(beside)
    greet(partner)
    pl.when(has_up)(lambda: greet(me + 4))
    pl.when(has_down)(lambda: greet(me - 4))
    for step in range(1, pairs):
        pl.semaphore_signal(
            barrier, inc=1, device_id={"pair": (core + step) % pairs}, device_id_type=MESH
        )
    for copy in loads:
        copy.start()
    pl.semaphore_wait(
        barrier, pairs + 1 + has_up.astype(jnp.int32) + has_down.astype(jnp.int32)
    )

    def first_copy(band, way, target):
        low, high = bands[band]
        start_row = (1 - hi) * half if way == PARTNER else hi * half
        return pltpu.make_async_remote_copy(
            src_ref=amps.at[pl.ds(start_row + low, high - low)],
            dst_ref=gath.at[me, pl.ds(low, high - low)],
            send_sem=send_sem.at[band, way, me], recv_sem=recv_sem.at[band, me],
            device_id={"vcol": target}, device_id_type=MESH,
        )

    def relay(source, band, way, target):
        low, high = bands[band]
        place = gath.at[source, pl.ds(low, high - low)]
        return pltpu.make_async_remote_copy(
            src_ref=place, dst_ref=place,
            send_sem=send_sem.at[band, way, source], recv_sem=recv_sem.at[band, source],
            device_id={"vcol": target}, device_id_type=MESH,
        )

    def panel_copy(step):
        return pltpu.make_async_remote_copy(
            src_ref=ints, dst_ref=panel.at[pl.ds(core * tiles, tiles)],
            send_sem=pair_send.at[step - 1], recv_sem=pair_recv.at[step - 1],
            device_id={"pair": (core + step) % pairs}, device_id_type=MESH,
        )

    def far_copy(source):
        return pltpu.make_async_remote_copy(
            src_ref=stage.at[source], dst_ref=far.at[KT_DEV * source + core % 2],
            send_sem=far_send.at[source], recv_sem=far_recv.at[source],
            device_id={"vcol": partner}, device_id_type=MESH,
        )

    def pass_copy(source, step, holder):
        slot = KT_DEV * source + holder % 2
        return pltpu.make_async_remote_copy(
            src_ref=far.at[slot], dst_ref=far.at[slot],
            send_sem=pass_send.at[step - 1, slot], recv_sem=pass_recv.at[slot],
            device_id={"pair": (core + step) % pairs}, device_id_type=MESH,
        )

    def if_holder(source, holder, action):
        if groups == 1:
            action()
        else:
            pl.when(source % groups == holder // 2)(action)

    def start(copy):
        copy.start()

    def wait_send(copy):
        copy.wait_send()

    def inside(at):
        return (at >= 0) & (at < length)

    def skipped(at):
        low = jnp.where(at % 2 == 0, at + 2, at - 1)
        high = jnp.where(at % 2 == 0, at + 1, at - 2)
        return jnp.where(at < length // 2, low, high)

    mate = line + 1 - 2 * (line % 2)
    skip, mate_skip = skipped(line), skipped(mate)

    def on_level(level, action):
        odd = level % 2
        h = hi + odd - 2 * hi * odd
        for x in (0, 1):
            d = level // 2 - x
            for away in (-1, 1):
                at = line + away * d
                valid = (d > 0 if away < 0 else d >= 0) & inside(at)
                if x == 1:
                    valid = valid & ((at != skip) | (odd == 0))
                pl.when(valid)(functools.partial(action, x, at, h, odd))

    def unit(at, h, x):
        return at * 4 + h * 2 + (1 - lo if x else lo)

    def onward(x, at, h, odd, band, action):
        source = unit(at, h, x)
        if x == 0:
            pl.when((at <= line) & has_up)(lambda: action(relay(source, band, UP, me + 4)))
            pl.when((at >= line) & has_down)(lambda: action(relay(source, band, DOWN, me - 4)))
            pl.when((at != skip) | (odd == 0))(
                lambda: action(relay(source, band, BESIDE, beside))
            )
        else:
            wanted = (at == mate_skip) & (odd == 1)
            pl.when(wanted & (mate > line))(lambda: action(relay(source, band, UP, me + 4)))
            pl.when(wanted & (mate < line))(lambda: action(relay(source, band, DOWN, me - 4)))

    def first_copies(action):
        for band in BANDS:
            action(first_copy(band, PARTNER, partner))
            pl.when(has_up)(lambda: action(first_copy(band, UP, me + 4)))
            pl.when(has_down)(lambda: action(first_copy(band, DOWN, me - 4)))
            action(first_copy(band, BESIDE, beside))

    def multiply(source, side, first, stop):
        tile_pair = (owner[KT_DEV * source], owner[KT_DEV * source + 1])
        home = partner if side else me
        rows = slice(first * PBLK, stop * PBLK)
        for slot, tile in enumerate(tile_pair):
            columns = slice(slot * TILE, (slot + 1) * TILE)
            for block in range(first, stop):
                part = slice(block * PBLK, (block + 1) * PBLK)
                value = gath[source, part, columns]
                for n in range(KT_DEV):
                    mark = screen[block, tile, KT_DEV * home + n].astype(jnp.float32)
                    lhs[n, part, columns] = value * jnp.full(value.shape, mark, jnp.float32).astype(
                        value.dtype
                    )
        if side:
            right = jnp.concatenate([far[KT_DEV * source], far[KT_DEV * source + 1]], axis=0)
        else:
            right = jnp.concatenate([panel[tile] for tile in tile_pair], axis=0)
        for n in range(KT_DEV):
            columns = slice(n * TILE, (n + 1) * TILE)
            place = slice((KT_DEV * side + n) * TILE, (KT_DEV * side + n + 1) * TILE)
            acc[rows, place] += jnp.dot(
                lhs[n, rows], right[:, columns], preferred_element_type=jnp.float32
            )

    first_copies(start)
    for step in range(1, pairs):
        panel_copy(step).start()
    acc[...] = jnp.zeros_like(acc)
    get_owner.wait()
    own_ints.wait()
    for step in range(1, pairs):
        panel_copy(step).wait_recv()

    def fill(source, _):
        if_holder(
            source, core,
            lambda: stage.__setitem__(source, panel[owner[KT_DEV * source + core % 2]]),
        )
        return 0

    def to_partner(action):
        def body(level, _):
            def send(x, at, h, odd):
                source = unit(at, 1 - h, x)
                if_holder(source, core, lambda: action(far_copy(source)))

            on_level(level, send)
            return 0

        lax.fori_loop(0, 2 * length + 2, body, 0)
        source = unit(skip, hi, 1)
        if_holder(source, core, lambda: action(far_copy(source)))

    lax.fori_loop(0, ranks, fill, 0)
    to_partner(start)

    def pass_on(source):
        def go():
            far_copy(source).wait_recv()
            for step in range(1, pairs):
                pass_copy(source, step, core).start()

        if_holder(source, core, go)

    def passed(source):
        for step in range(1, pairs):
            holder = (core + step) % pairs
            if_holder(
                source, holder, lambda: pass_copy(source, step, holder).wait_recv()
            )

    def arrived(source, band):
        relay(source, band, BESIDE, beside).wait_recv()

    def far_whole(source):
        passed(source)
        multiply(source, 1, 0, blocks)

    def find(slot, _):
        tile = owner[slot]
        row, col = (tile >> 2) & 1, (tile >> 1) & 1
        place[slot] = (tile & -8) | (col << 2) | ((row ^ hi) << 1) | (tile & 1)
        return 0

    lax.fori_loop(0, KT_DEV * ranks, find, 0)
    get_screen.wait()
    own_amps.wait()
    multiply(me, 0, 0, blocks)

    def on_unit(action):
        return lambda x, at, h, odd: action(unit(at, h, x))

    def relay_level(level):
        for band in BANDS:

            def take(x, at, h, odd):
                arrived(unit(at, h, x), band)
                onward(x, at, h, odd, band, start)

            on_level(level, take)

    def near_level(level):
        on_level(level, on_unit(lambda source: multiply(source, 0, 0, blocks)))

    final = 2 * length + 1
    skipped_unit = unit(skip, 1 - hi, 1)
    outer = (line == 0) | (line == length - 1)
    lag = jnp.where(outer, 1, 2)

    def early_level(level, _):
        relay_level(level)
        on_level(level - lag, on_unit(pass_on))
        near_level(level)
        on_level(level - lag, on_unit(far_whole))
        return 0

    def late_level(level, _):
        on_level(level, on_unit(pass_on))
        relay_level(level)
        near_level(level)
        on_level(level - 1, on_unit(far_whole))
        return 0

    lax.fori_loop(1, final - 2, early_level, 0)

    spot_in_plane = line * 2 + lo

    flips = [1 - 2 * lo, 2 * (1 - 2 * hi)]
    for bit in range(length.bit_length() - 1):
        flips.append((4 << bit) * (1 - 2 * ((line // (1 << bit)) % 2)))

    def moved(mask):
        return sum(flip for bit, flip in enumerate(flips) if mask >> bit & 1)

    def whole(buffer, count, send, recv):
        place = buffer.at[pl.ds(0, count)]
        return pltpu.make_async_remote_copy(
            src_ref=place, dst_ref=place, send_sem=send, recv_sem=recv,
            device_id={"vcol": beside}, device_id_type=MESH,
        )

    def send_slots(band):
        for mask in reversed(range(1, ranks)):
            target = me + moved(mask)
            pltpu.make_async_remote_copy(
                src_ref=slots[band].at[target], dst_ref=landed[band].at[me],
                send_sem=back_send.at[band], recv_sem=back_recv.at[band],
                device_id={"vcol": target}, device_id_type=MESH,
            ).start()

    def send_parts(side, band):
        for mask in reversed(range(1, ranks)):
            if mask & 2 == 0:
                target = me + moved(mask)
                column = spot_in_plane + moved(mask & 1) + moved(mask & -4) // 2
                pltpu.make_async_remote_copy(
                    src_ref=parts[band].at[side, column],
                    dst_ref=natural[band].at[
                        pl.ds((spot_in_plane * 2 + side) * KT_DEV, KT_DEV)
                    ],
                    send_sem=out_send.at[side, band], recv_sem=out_recv.at[band],
                    device_id={"vcol": target}, device_id_type=MESH,
                ).start()

    def parts_taken(band):
        return whole(
            natural[band], (plane - 1) * 2 * KT_DEV, out_send.at[0, band], out_recv.at[band]
        )

    def parts_sent(side, band):
        return whole(
            parts[band].at[side], plane - 1, out_send.at[side, band], out_recv.at[band]
        )

    def slots_moved(band):
        return whole(slots[band], ranks - 1, back_send.at[band], back_recv.at[band])

    def send_out(side, band):
        low, high = bands[band]
        part = (high - low) // plane
        for i in range(plane):
            for n in range(KT_DEV):
                column = (side * KT_DEV + n) * TILE
                parts[band][side, i, n] = acc[
                    low + i * part : low + (i + 1) * part, column : column + TILE
                ].astype(jnp.bfloat16)
        send_parts(side, band)
        natural[band][pl.ds((spot_in_plane * 2 + side) * KT_DEV, KT_DEV)] = parts[band][
            side, spot_in_plane
        ]

    @pl.when(outer)
    def _():
        on_level(final - 3, on_unit(pass_on))
        lax.fori_loop(final - 2, final, late_level, 0)
        on_level(final, on_unit(pass_on))
        pass_on(skipped_unit)
        on_level(final - 1, on_unit(far_whole))
        on_level(final, on_unit(passed))
        passed(skipped_unit)
        for band in BANDS:
            low, high = bands[band]

            def finish(source):
                arrived(source, band)
                for side in (0, 1):
                    multiply(source, side, low // PBLK, high // PBLK)

            on_level(final, on_unit(finish))
            finish(skipped_unit)
            for side in (0, 1):
                send_out(side, band)

    @pl.when(~outer)
    def _():
        relay_level(final - 2)
        near_level(final - 2)
        for band in BANDS:
            arrived(skipped_unit, band)
        multiply(skipped_unit, 0, 0, blocks)
        for band in BANDS:
            send_out(0, band)

        def rest(level, _):
            on_level(level, on_unit(pass_on))
            on_level(level - 1, on_unit(far_whole))
            return 0

        on_level(final - 4, on_unit(pass_on))
        lax.fori_loop(final - 3, final - 1, rest, 0)
        pass_on(skipped_unit)
        on_level(final - 2, on_unit(far_whole))
        passed(skipped_unit)
        for band in BANDS:
            low, high = bands[band]
            multiply(skipped_unit, 1, low // PBLK, high // PBLK)
            send_out(1, band)

    get_occ.wait()
    get_virt.wait()
    get_mine.wait()
    rows = mine.shape[0]
    eye = lax.broadcasted_iota(jnp.int32, (TILE, TILE), 0) == lax.broadcasted_iota(
        jnp.int32, (TILE, TILE), 1
    )
    for g in range(rows // TILE):
        part = slice(g * TILE, (g + 1) * TILE)
        spread = jnp.broadcast_to(occ[g : g + 1, :], (TILE, TILE))
        column = jnp.sum(jnp.where(eye, spread, 0.0), axis=1, keepdims=True)
        for n in range(KT_DEV):
            columns = slice(n * TILE, (n + 1) * TILE)
            level = virt[pl.ds(owner[KT_DEV * me + n], 1), :]
            base[part, columns] = (level - column) * mine[part, columns].astype(jnp.float32)

    for band in BANDS:
        parts_taken(band).wait_recv()
        for j in range(ranks):
            for n in range(KT_DEV):
                slots[band][j, n] = natural[band][place[KT_DEV * j + n]]
        send_slots(band)
        landed[band][me] = slots[band][me]

    first_copies(wait_send)

    def drain(level, _):
        for band in BANDS:
            on_level(
                level, lambda x, at, h, odd: onward(x, at, h, odd, band, wait_send)
            )
        return 0

    lax.fori_loop(1, final + 1, drain, 0)
    to_partner(wait_send)

    def close(source, _):
        def go():
            for step in range(1, pairs):
                pass_copy(source, step, core).wait_send()

        if_holder(source, core, go)
        return 0

    lax.fori_loop(0, ranks, close, 0)
    for step in range(1, pairs):
        panel_copy(step).wait_send()
    for band in BANDS:
        for side in (0, 1):
            parts_sent(side, band).wait_send()

    for band in BANDS:
        low, high = bands[band]
        part = (high - low) // plane
        slots_moved(band).wait_recv()
        for j in range(ranks):
            at = ((j % 4) // 2) * half + low + ((j // 4) * 2 + j % 2) * part
            for n in range(KT_DEV):
                columns = slice(n * TILE, (n + 1) * TILE)
                out[at : at + part, columns] = (
                    landed[band][j, n].astype(jnp.float32) + base[at : at + part, columns]
                ).astype(out.dtype)
    for band in BANDS:
        slots_moved(band).wait_send()


def local(ranks, pairs, amplitudes, tile_owner, integrals, screening, occ_energy, virt_energy):
    rows, width = amplitudes.shape
    tiles = integrals.shape[0] // TILE
    count = tile_owner.shape[0]
    half, plane = rows // 2, ranks // 2
    blocks = half // PBLK
    hbm = pl.BlockSpec(memory_space=pl.ANY)
    dma = pltpu.SemaphoreType.DMA
    sizes = [(high - low) // plane for low, high in band_edges(half)]

    def exchange(lead):
        return [pltpu.VMEM((*lead, size, TILE), jnp.bfloat16) for size in sizes]

    return pl.pallas_call(
        functools.partial(ladder_kernel, ranks, pairs),
        out_shape=pltpu.VMEM((rows, width), jnp.bfloat16),
        in_specs=[hbm] * 6,
        out_specs=pl.BlockSpec(memory_space=pltpu.VMEM),
        scratch_shapes=[
            pltpu.SMEM((count,), jnp.int32),
            pltpu.SMEM((count,), jnp.int32),
            pltpu.SMEM((blocks, count, count), jnp.int32),
            pltpu.VMEM((rows // TILE, TILE), jnp.float32),
            pltpu.VMEM((count, TILE), jnp.float32),
            pltpu.VMEM((rows, width), jnp.bfloat16),
            pltpu.VMEM((rows, width), jnp.float32),
            pltpu.VMEM((ranks, half, width), jnp.bfloat16),
            pltpu.VMEM((tiles * pairs, TILE, width), jnp.bfloat16),
            pltpu.VMEM((ranks, TILE, width), jnp.bfloat16),
            pltpu.VMEM((KT_DEV * ranks, TILE, width), jnp.bfloat16),
            pltpu.VMEM((KT_DEV, half, width), jnp.bfloat16),
            pltpu.VMEM((half, 2 * width), jnp.float32),
            exchange((2, plane, KT_DEV)),
            exchange((plane * 2 * KT_DEV,)),
            exchange((ranks, KT_DEV)),
            exchange((ranks, KT_DEV)),
            dma((7,)),
            dma((len(BANDS), 4, ranks)),
            dma((len(BANDS), ranks)),
            dma((pairs - 1,)),
            dma((pairs - 1,)),
            dma((ranks,)),
            dma((ranks,)),
            dma((pairs - 1, KT_DEV * ranks)),
            dma((KT_DEV * ranks,)),
            dma((2, len(BANDS))),
            dma((len(BANDS),)),
            dma((len(BANDS),)),
            dma((len(BANDS),)),
        ],
        compiler_params=pltpu.CompilerParams(
            collective_id=0, has_side_effects=True, vmem_limit_bytes=62 * 1024 * 1024
        ),
    )(
        amplitudes,
        tile_owner,
        integrals.reshape(tiles, TILE, width),
        screening,
        occ_energy.reshape(rows // TILE, TILE),
        virt_energy.reshape(count, TILE),
    )


def solution(mesh):
    return jax.shard_map(
        functools.partial(local, mesh.shape["vcol"], mesh.shape["pair"]),
        mesh=mesh,
        in_specs=(P("pair", "vcol"), P(), P("pair", "vcol"), P("pair", None, None), P("pair"), P()),
        out_specs=P("pair", "vcol"),
        check_vma=False,
    )
```

```python
import functools

import jax
import jax.numpy as jnp
from jax import lax
from jax.experimental import pallas as pl
from jax.experimental.pallas import tpu as pltpu
from jax.sharding import PartitionSpec as P

TILE = 128
PBLK = 64
KT_DEV = 2
MESH = pl.DeviceIdType.MESH
UP, DOWN, BESIDE, PARTNER = 0, 1, 2, 3
SHARES, LEGS = (2,), (2,)
BANDS, HAULS = range(len(SHARES) + 1), range(len(LEGS) + 1)


def band_edges(half, shares):
    blocks = half // PBLK
    edges = [0, *(blocks * share // 5 * PBLK for share in shares), half]
    return tuple(zip(edges[:-1], edges[1:]))


def ladder_kernel(
    ranks, pairs, amps, owner_in, ints, screen_in, occ_in, virt_in, out,
    owner, place, screen, occ, virt, mine, base, gath, panel, stage, far, lhs, acc,
    parts, natural, slots, landed,
    local_sem, send_sem, recv_sem, pair_send, pair_recv, far_send, far_recv, pass_send, pass_recv,
    out_send, out_recv, back_send, back_recv,
):
    length = ranks // 4
    plane = ranks // 2
    groups = pairs // 2
    me = lax.axis_index("vcol")
    core = lax.axis_index("pair")
    line, spot = me // 4, me % 4
    hi, lo = spot // 2, spot % 2
    beside = line * 4 + hi * 2 + (1 - lo)
    partner = line * 4 + (1 - hi) * 2 + lo
    has_up, has_down = line < length - 1, line > 0
    half = gath.shape[1]
    blocks = half // PBLK
    tiles = ints.shape[0]
    bands, hauls = band_edges(half, SHARES), band_edges(half, LEGS)

    def load(index, source, target):
        return pltpu.make_async_copy(source, target, local_sem.at[index])

    own_ints = load(0, ints, panel.at[pl.ds(core * tiles, tiles)])
    own_amps = load(1, amps.at[pl.ds(hi * half, half)], gath.at[me])
    get_owner = load(2, owner_in, owner)
    get_screen = load(3, screen_in.at[pl.ds(hi * blocks, blocks)], screen)
    get_occ = load(4, occ_in, occ)
    get_virt = load(5, virt_in, virt)
    get_mine = load(6, amps, mine)
    loads = (get_owner, own_ints, get_screen, own_amps, get_occ, get_virt, get_mine)

    barrier = pltpu.get_barrier_semaphore()

    def greet(target):
        pl.semaphore_signal(barrier, inc=1, device_id={"vcol": target}, device_id_type=MESH)

    greet(beside)
    greet(partner)
    pl.when(has_up)(lambda: greet(me + 4))
    pl.when(has_down)(lambda: greet(me - 4))
    for step in range(1, pairs):
        pl.semaphore_signal(
            barrier, inc=1, device_id={"pair": (core + step) % pairs}, device_id_type=MESH
        )
    for copy in loads:
        copy.start()
    pl.semaphore_wait(
        barrier, pairs + 1 + has_up.astype(jnp.int32) + has_down.astype(jnp.int32)
    )

    def first_copy(band, way, target):
        low, high = hauls[band]
        start_row = (1 - hi) * half if way == PARTNER else hi * half
        return pltpu.make_async_remote_copy(
            src_ref=amps.at[pl.ds(start_row + low, high - low)],
            dst_ref=gath.at[me, pl.ds(low, high - low)],
            send_sem=send_sem.at[band, way, me], recv_sem=recv_sem.at[band, me],
            device_id={"vcol": target}, device_id_type=MESH,
        )

    def relay(source, band, way, target):
        low, high = hauls[band]
        place = gath.at[source, pl.ds(low, high - low)]
        return pltpu.make_async_remote_copy(
            src_ref=place, dst_ref=place,
            send_sem=send_sem.at[band, way, source], recv_sem=recv_sem.at[band, source],
            device_id={"vcol": target}, device_id_type=MESH,
        )

    def panel_copy(step):
        return pltpu.make_async_remote_copy(
            src_ref=ints, dst_ref=panel.at[pl.ds(core * tiles, tiles)],
            send_sem=pair_send.at[step - 1], recv_sem=pair_recv.at[step - 1],
            device_id={"pair": (core + step) % pairs}, device_id_type=MESH,
        )

    def far_copy(source):
        return pltpu.make_async_remote_copy(
            src_ref=stage.at[source], dst_ref=far.at[KT_DEV * source + core % 2],
            send_sem=far_send.at[source], recv_sem=far_recv.at[source],
            device_id={"vcol": partner}, device_id_type=MESH,
        )

    def pass_copy(source, step, holder):
        slot = KT_DEV * source + holder % 2
        return pltpu.make_async_remote_copy(
            src_ref=far.at[slot], dst_ref=far.at[slot],
            send_sem=pass_send.at[step - 1, slot], recv_sem=pass_recv.at[slot],
            device_id={"pair": (core + step) % pairs}, device_id_type=MESH,
        )

    def if_holder(source, holder, action):
        if groups == 1:
            action()
        else:
            pl.when(source % groups == holder // 2)(action)

    def start(copy):
        copy.start()

    def wait_send(copy):
        copy.wait_send()

    def inside(at):
        return (at >= 0) & (at < length)

    def skipped(at):
        low = jnp.where(at % 2 == 0, at + 2, at - 1)
        high = jnp.where(at % 2 == 0, at + 1, at - 2)
        return jnp.where(at < length // 2, low, high)

    mate = line + 1 - 2 * (line % 2)
    skip, mate_skip = skipped(line), skipped(mate)

    def on_level(level, action):
        odd = level % 2
        h = hi + odd - 2 * hi * odd
        for x in (0, 1):
            d = level // 2 - x
            for away in (-1, 1):
                at = line + away * d
                valid = (d > 0 if away < 0 else d >= 0) & inside(at)
                if x == 1:
                    valid = valid & ((at != skip) | (odd == 0))
                pl.when(valid)(functools.partial(action, x, at, h, odd))

    def unit(at, h, x):
        return at * 4 + h * 2 + (1 - lo if x else lo)

    def onward(x, at, h, odd, band, action):
        source = unit(at, h, x)
        if x == 0:
            pl.when((at <= line) & has_up)(lambda: action(relay(source, band, UP, me + 4)))
            pl.when((at >= line) & has_down)(lambda: action(relay(source, band, DOWN, me - 4)))
            pl.when((at != skip) | (odd == 0))(
                lambda: action(relay(source, band, BESIDE, beside))
            )
        else:
            wanted = (at == mate_skip) & (odd == 1)
            pl.when(wanted & (mate > line))(lambda: action(relay(source, band, UP, me + 4)))
            pl.when(wanted & (mate < line))(lambda: action(relay(source, band, DOWN, me - 4)))

    def first_copies(action):
        for band in HAULS:
            action(first_copy(band, PARTNER, partner))
            pl.when(has_up)(lambda: action(first_copy(band, UP, me + 4)))
            pl.when(has_down)(lambda: action(first_copy(band, DOWN, me - 4)))
            action(first_copy(band, BESIDE, beside))

    def multiply(source, side, first, stop):
        tile_pair = (owner[KT_DEV * source], owner[KT_DEV * source + 1])
        home = partner if side else me
        rows = slice(first * PBLK, stop * PBLK)
        for slot, tile in enumerate(tile_pair):
            columns = slice(slot * TILE, (slot + 1) * TILE)
            for block in range(first, stop):
                part = slice(block * PBLK, (block + 1) * PBLK)
                value = gath[source, part, columns]
                for n in range(KT_DEV):
                    mark = screen[block, tile, KT_DEV * home + n].astype(jnp.float32)
                    lhs[n, part, columns] = value * jnp.full(value.shape, mark, jnp.float32).astype(
                        value.dtype
                    )
        if side:
            right = jnp.concatenate([far[KT_DEV * source], far[KT_DEV * source + 1]], axis=0)
        else:
            right = jnp.concatenate([panel[tile] for tile in tile_pair], axis=0)
        for n in range(KT_DEV):
            columns = slice(n * TILE, (n + 1) * TILE)
            place = slice((KT_DEV * side + n) * TILE, (KT_DEV * side + n + 1) * TILE)
            acc[rows, place] += jnp.dot(
                lhs[n, rows], right[:, columns], preferred_element_type=jnp.float32
            )

    first_copies(start)
    for step in range(1, pairs):
        panel_copy(step).start()
    acc[...] = jnp.zeros_like(acc)
    get_owner.wait()
    own_ints.wait()
    for step in range(1, pairs):
        panel_copy(step).wait_recv()

    def fill(source, _):
        if_holder(
            source, core,
            lambda: stage.__setitem__(source, panel[owner[KT_DEV * source + core % 2]]),
        )
        return 0

    def to_partner(action, first, stop):
        def body(level, _):
            def send(x, at, h, odd):
                source = unit(at, 1 - h, x)
                if_holder(source, core, lambda: action(far_copy(source)))

            on_level(level, send)
            return 0

        lax.fori_loop(first, stop, body, 0)

    def skipped_to_partner(action):
        source = unit(skip, hi, 1)
        if_holder(source, core, lambda: action(far_copy(source)))

    lax.fori_loop(0, ranks, fill, 0)
    to_partner(start, 0, 3)

    def pass_on(source):
        def go():
            far_copy(source).wait_recv()
            for step in range(1, pairs):
                pass_copy(source, step, core).start()

        if_holder(source, core, go)

    def passed(source):
        for step in range(1, pairs):
            holder = (core + step) % pairs
            if_holder(
                source, holder, lambda: pass_copy(source, step, holder).wait_recv()
            )

    def arrived(source, band):
        relay(source, band, BESIDE, beside).wait_recv()

    def far_whole(source):
        passed(source)
        multiply(source, 1, 0, blocks)

    def on_unit(action):
        return lambda x, at, h, odd: action(unit(at, h, x))

    def relay_level(level):
        for band in HAULS:

            def take(x, at, h, odd):
                arrived(unit(at, h, x), band)
                onward(x, at, h, odd, band, start)

            on_level(level, take)

    def near_level(level):
        on_level(level, on_unit(lambda source: multiply(source, 0, 0, blocks)))

    final = 2 * length + 1
    skipped_unit = unit(skip, 1 - hi, 1)
    outer = (line == 0) | (line == length - 1)
    lag = jnp.where(outer, 1, 2)

    def early_level(level, _):
        pl.when(level > 1)(lambda: relay_level(level))
        on_level(level - lag, on_unit(pass_on))
        near_level(level)
        on_level(level - lag, on_unit(far_whole))
        return 0

    def late_level(level, _):
        on_level(level, on_unit(pass_on))
        relay_level(level)
        near_level(level)
        on_level(level - 1, on_unit(far_whole))
        return 0

    relay_level(1)
    to_partner(start, 3, 2 * length + 2)
    skipped_to_partner(start)
    get_screen.wait()
    own_amps.wait()
    multiply(me, 0, 0, blocks)
    lax.fori_loop(1, final - 2, early_level, 0)

    spot_in_plane = line * 2 + lo

    flips = [1 - 2 * lo, 2 * (1 - 2 * hi)]
    for bit in range(length.bit_length() - 1):
        flips.append((4 << bit) * (1 - 2 * ((line // (1 << bit)) % 2)))

    def moved(mask):
        return sum(flip for bit, flip in enumerate(flips) if mask >> bit & 1)

    def whole(buffer, count, send, recv):
        place = buffer.at[pl.ds(0, count)]
        return pltpu.make_async_remote_copy(
            src_ref=place, dst_ref=place, send_sem=send, recv_sem=recv,
            device_id={"vcol": beside}, device_id_type=MESH,
        )

    def send_slots(band):
        for mask in reversed(range(1, ranks)):
            target = me + moved(mask)
            pltpu.make_async_remote_copy(
                src_ref=slots[band].at[target], dst_ref=landed[band].at[me],
                send_sem=back_send.at[band], recv_sem=back_recv.at[band],
                device_id={"vcol": target}, device_id_type=MESH,
            ).start()

    def send_parts(side, band):
        for mask in reversed(range(1, ranks)):
            if mask & 2 == 0:
                target = me + moved(mask)
                column = spot_in_plane + moved(mask & 1) + moved(mask & -4) // 2
                pltpu.make_async_remote_copy(
                    src_ref=parts[band].at[side, column],
                    dst_ref=natural[band].at[
                        pl.ds((spot_in_plane * 2 + side) * KT_DEV, KT_DEV)
                    ],
                    send_sem=out_send.at[side, band], recv_sem=out_recv.at[band],
                    device_id={"vcol": target}, device_id_type=MESH,
                ).start()

    def parts_taken(band):
        return whole(
            natural[band], (plane - 1) * 2 * KT_DEV, out_send.at[0, band], out_recv.at[band]
        )

    def parts_sent(side, band):
        return whole(
            parts[band].at[side], plane - 1, out_send.at[side, band], out_recv.at[band]
        )

    def slots_moved(band):
        return whole(slots[band], ranks - 1, back_send.at[band], back_recv.at[band])

    def send_out(side, band):
        low, high = bands[band]
        part = (high - low) // plane
        for i in range(plane):
            for n in range(KT_DEV):
                column = (side * KT_DEV + n) * TILE
                parts[band][side, i, n] = acc[
                    low + i * part : low + (i + 1) * part, column : column + TILE
                ].astype(jnp.bfloat16)
        send_parts(side, band)
        natural[band][pl.ds((spot_in_plane * 2 + side) * KT_DEV, KT_DEV)] = parts[band][
            side, spot_in_plane
        ]

    @pl.when(outer)
    def _():
        on_level(final - 3, on_unit(pass_on))
        lax.fori_loop(final - 2, final, late_level, 0)
        on_level(final, on_unit(pass_on))
        pass_on(skipped_unit)
        on_level(final - 1, on_unit(far_whole))
        on_level(final, on_unit(passed))
        passed(skipped_unit)
        for band in BANDS:
            low, high = bands[band]

            def finish(source):
                for haul, (top, _) in enumerate(hauls):
                    if low <= top < high:
                        arrived(source, haul)

            on_level(final, on_unit(finish))
            finish(skipped_unit)
            for side in (0, 1):
                part = functools.partial(
                    multiply, side=side, first=low // PBLK, stop=high // PBLK
                )
                on_level(final, on_unit(part))
                part(skipped_unit)
                send_out(side, band)

    @pl.when(~outer)
    def _():
        relay_level(final - 2)
        near_level(final - 2)
        for band in HAULS:
            arrived(skipped_unit, band)
        multiply(skipped_unit, 0, 0, blocks)
        for band in BANDS:
            send_out(0, band)

        def rest(level, _):
            on_level(level, on_unit(pass_on))
            on_level(level - 1, on_unit(far_whole))
            return 0

        on_level(final - 4, on_unit(pass_on))
        lax.fori_loop(final - 3, final - 1, rest, 0)
        pass_on(skipped_unit)
        on_level(final - 2, on_unit(far_whole))
        passed(skipped_unit)
        for band in BANDS:
            low, high = bands[band]
            multiply(skipped_unit, 1, low // PBLK, high // PBLK)
            send_out(1, band)

    def find(slot, _):
        tile = owner[slot]
        row, col = (tile >> 2) & 1, (tile >> 1) & 1
        place[slot] = (tile & -8) | (col << 2) | ((row ^ hi) << 1) | (tile & 1)
        return 0

    lax.fori_loop(0, KT_DEV * ranks, find, 0)
    get_occ.wait()
    get_virt.wait()
    get_mine.wait()
    rows = mine.shape[0]
    eye = lax.broadcasted_iota(jnp.int32, (TILE, TILE), 0) == lax.broadcasted_iota(
        jnp.int32, (TILE, TILE), 1
    )
    for g in range(rows // TILE):
        part = slice(g * TILE, (g + 1) * TILE)
        spread = jnp.broadcast_to(occ[g : g + 1, :], (TILE, TILE))
        column = jnp.sum(jnp.where(eye, spread, 0.0), axis=1, keepdims=True)
        for n in range(KT_DEV):
            columns = slice(n * TILE, (n + 1) * TILE)
            level = virt[pl.ds(owner[KT_DEV * me + n], 1), :]
            base[part, columns] = (level - column) * mine[part, columns].astype(jnp.float32)

    for band in BANDS:
        parts_taken(band).wait_recv()
        for j in range(ranks):
            for n in range(KT_DEV):
                slots[band][j, n] = natural[band][place[KT_DEV * j + n]]
        send_slots(band)
        landed[band][me] = slots[band][me]

    first_copies(wait_send)

    def drain(level, _):
        for band in HAULS:
            on_level(
                level, lambda x, at, h, odd: onward(x, at, h, odd, band, wait_send)
            )
        return 0

    lax.fori_loop(1, final + 1, drain, 0)
    to_partner(wait_send, 0, 2 * length + 2)
    skipped_to_partner(wait_send)

    def close(source, _):
        def go():
            for step in range(1, pairs):
                pass_copy(source, step, core).wait_send()

        if_holder(source, core, go)
        return 0

    lax.fori_loop(0, ranks, close, 0)
    for step in range(1, pairs):
        panel_copy(step).wait_send()
    for band in BANDS:
        for side in (0, 1):
            parts_sent(side, band).wait_send()

    for band in BANDS:
        low, high = bands[band]
        part = (high - low) // plane
        slots_moved(band).wait_recv()
        for j in range(ranks):
            at = ((j % 4) // 2) * half + low + ((j // 4) * 2 + j % 2) * part
            for n in range(KT_DEV):
                columns = slice(n * TILE, (n + 1) * TILE)
                out[at : at + part, columns] = (
                    landed[band][j, n].astype(jnp.float32) + base[at : at + part, columns]
                ).astype(out.dtype)
    for band in BANDS:
        slots_moved(band).wait_send()


def local(ranks, pairs, amplitudes, tile_owner, integrals, screening, occ_energy, virt_energy):
    rows, width = amplitudes.shape
    tiles = integrals.shape[0] // TILE
    count = tile_owner.shape[0]
    half, plane = rows // 2, ranks // 2
    blocks = half // PBLK
    hbm = pl.BlockSpec(memory_space=pl.ANY)
    dma = pltpu.SemaphoreType.DMA
    sizes = [(high - low) // plane for low, high in band_edges(half, SHARES)]

    def exchange(lead):
        return [pltpu.VMEM((*lead, size, TILE), jnp.bfloat16) for size in sizes]

    return pl.pallas_call(
        functools.partial(ladder_kernel, ranks, pairs),
        out_shape=pltpu.VMEM((rows, width), jnp.bfloat16),
        in_specs=[hbm] * 6,
        out_specs=pl.BlockSpec(memory_space=pltpu.VMEM),
        scratch_shapes=[
            pltpu.SMEM((count,), jnp.int32),
            pltpu.SMEM((count,), jnp.int32),
            pltpu.SMEM((blocks, count, count), jnp.int32),
            pltpu.VMEM((rows // TILE, TILE), jnp.float32),
            pltpu.VMEM((count, TILE), jnp.float32),
            pltpu.VMEM((rows, width), jnp.bfloat16),
            pltpu.VMEM((rows, width), jnp.float32),
            pltpu.VMEM((ranks, half, width), jnp.bfloat16),
            pltpu.VMEM((tiles * pairs, TILE, width), jnp.bfloat16),
            pltpu.VMEM((ranks, TILE, width), jnp.bfloat16),
            pltpu.VMEM((KT_DEV * ranks, TILE, width), jnp.bfloat16),
            pltpu.VMEM((KT_DEV, half, width), jnp.bfloat16),
            pltpu.VMEM((half, 2 * width), jnp.float32),
            exchange((2, plane, KT_DEV)),
            exchange((plane * 2 * KT_DEV,)),
            exchange((ranks, KT_DEV)),
            exchange((ranks, KT_DEV)),
            dma((7,)),
            dma((len(HAULS), 4, ranks)),
            dma((len(HAULS), ranks)),
            dma((pairs - 1,)),
            dma((pairs - 1,)),
            dma((ranks,)),
            dma((ranks,)),
            dma((pairs - 1, KT_DEV * ranks)),
            dma((KT_DEV * ranks,)),
            dma((2, len(BANDS))),
            dma((len(BANDS),)),
            dma((len(BANDS),)),
            dma((len(BANDS),)),
        ],
        compiler_params=pltpu.CompilerParams(
            collective_id=0, has_side_effects=True, vmem_limit_bytes=62 * 1024 * 1024
        ),
    )(
        amplitudes,
        tile_owner,
        integrals.reshape(tiles, TILE, width),
        screening,
        occ_energy.reshape(rows // TILE, TILE),
        virt_energy.reshape(count, TILE),
    )


def solution(mesh):
    return jax.shard_map(
        functools.partial(local, mesh.shape["vcol"], mesh.shape["pair"]),
        mesh=mesh,
        in_specs=(P("pair", "vcol"), P(), P("pair", "vcol"), P("pair", None, None), P("pair"), P()),
        out_specs=P("pair", "vcol"),
        check_vma=False,
    )
```

```python
import functools

import jax
import jax.numpy as jnp
from jax import lax
from jax.experimental import pallas as pl
from jax.experimental.pallas import tpu as pltpu
from jax.sharding import PartitionSpec as P

TILE = 128
PBLK = 64
KT_DEV = 2
MESH = pl.DeviceIdType.MESH
UP, DOWN, BESIDE, PARTNER = 0, 1, 2, 3
SHARES, LEGS = (2,), (2,)
BANDS, HAULS = range(len(SHARES) + 1), range(len(LEGS) + 1)


def band_edges(half, shares):
    blocks = half // PBLK
    edges = [0, *(blocks * share // 5 * PBLK for share in shares), half]
    return tuple(zip(edges[:-1], edges[1:]))


def ladder_kernel(
    ranks, pairs, amps, owner_in, ints, screen_in, occ_in, virt_in, out,
    owner, place, screen, occ, virt, mine, base, gath, panel, stage, far, lhs, acc,
    parts, natural, slots, landed,
    local_sem, send_sem, recv_sem, pair_send, pair_recv, far_send, far_recv, pass_send, pass_recv,
    out_send, out_recv, back_send, back_recv,
):
    length = ranks // 4
    plane = ranks // 2
    groups = pairs // 2
    me = lax.axis_index("vcol")
    core = lax.axis_index("pair")
    line, spot = me // 4, me % 4
    hi, lo = spot // 2, spot % 2
    beside = line * 4 + hi * 2 + (1 - lo)
    partner = line * 4 + (1 - hi) * 2 + lo
    has_up, has_down = line < length - 1, line > 0
    half = gath.shape[1]
    blocks = half // PBLK
    tiles = ints.shape[0]
    bands, hauls = band_edges(half, SHARES), band_edges(half, LEGS)

    def load(index, source, target):
        return pltpu.make_async_copy(source, target, local_sem.at[index])

    own_ints = load(0, ints, panel.at[pl.ds(core * tiles, tiles)])
    own_amps = load(1, amps.at[pl.ds(hi * half, half)], gath.at[me])
    get_owner = load(2, owner_in, owner)
    get_screen = load(3, screen_in.at[pl.ds(hi * blocks, blocks)], screen)
    get_occ = load(4, occ_in, occ)
    get_virt = load(5, virt_in, virt)
    get_mine = load(6, amps, mine)
    loads = (get_owner, own_ints, get_screen, own_amps, get_occ, get_virt, get_mine)

    barrier = pltpu.get_barrier_semaphore()

    def greet(target):
        pl.semaphore_signal(barrier, inc=1, device_id={"vcol": target}, device_id_type=MESH)

    greet(beside)
    greet(partner)
    pl.when(has_up)(lambda: greet(me + 4))
    pl.when(has_down)(lambda: greet(me - 4))
    for step in range(1, pairs):
        pl.semaphore_signal(
            barrier, inc=1, device_id={"pair": (core + step) % pairs}, device_id_type=MESH
        )
    for copy in loads:
        copy.start()
    pl.semaphore_wait(
        barrier, pairs + 1 + has_up.astype(jnp.int32) + has_down.astype(jnp.int32)
    )

    def first_copy(band, way, target):
        low, high = hauls[band]
        start_row = (1 - hi) * half if way == PARTNER else hi * half
        return pltpu.make_async_remote_copy(
            src_ref=amps.at[pl.ds(start_row + low, high - low)],
            dst_ref=gath.at[me, pl.ds(low, high - low)],
            send_sem=send_sem.at[band, way, me], recv_sem=recv_sem.at[band, me],
            device_id={"vcol": target}, device_id_type=MESH,
        )

    def relay(source, band, way, target):
        low, high = hauls[band]
        place = gath.at[source, pl.ds(low, high - low)]
        return pltpu.make_async_remote_copy(
            src_ref=place, dst_ref=place,
            send_sem=send_sem.at[band, way, source], recv_sem=recv_sem.at[band, source],
            device_id={"vcol": target}, device_id_type=MESH,
        )

    def panel_copy(step):
        return pltpu.make_async_remote_copy(
            src_ref=ints, dst_ref=panel.at[pl.ds(core * tiles, tiles)],
            send_sem=pair_send.at[step - 1], recv_sem=pair_recv.at[step - 1],
            device_id={"pair": (core + step) % pairs}, device_id_type=MESH,
        )

    def far_copy(source):
        return pltpu.make_async_remote_copy(
            src_ref=stage.at[source], dst_ref=far.at[KT_DEV * source + core % 2],
            send_sem=far_send.at[source], recv_sem=far_recv.at[source],
            device_id={"vcol": partner}, device_id_type=MESH,
        )

    def pass_copy(source, step, holder):
        slot = KT_DEV * source + holder % 2
        return pltpu.make_async_remote_copy(
            src_ref=far.at[slot], dst_ref=far.at[slot],
            send_sem=pass_send.at[step - 1, slot], recv_sem=pass_recv.at[slot],
            device_id={"pair": (core + step) % pairs}, device_id_type=MESH,
        )

    def if_holder(source, holder, action):
        if groups == 1:
            action()
        else:
            pl.when(source % groups == holder // 2)(action)

    def start(copy):
        copy.start()

    def wait_send(copy):
        copy.wait_send()

    def inside(at):
        return (at >= 0) & (at < length)

    def skipped(at):
        low = jnp.where(at % 2 == 0, at + 2, at - 1)
        high = jnp.where(at % 2 == 0, at + 1, at - 2)
        return jnp.where(at < length // 2, low, high)

    mate = line + 1 - 2 * (line % 2)
    skip, mate_skip = skipped(line), skipped(mate)

    def on_level(level, action):
        odd = level % 2
        h = hi + odd - 2 * hi * odd
        for x in (0, 1):
            d = level // 2 - x
            for away in (-1, 1):
                at = line + away * d
                valid = (d > 0 if away < 0 else d >= 0) & inside(at)
                if x == 1:
                    valid = valid & ((at != skip) | (odd == 0))
                pl.when(valid)(functools.partial(action, x, at, h, odd))

    def unit(at, h, x):
        return at * 4 + h * 2 + (1 - lo if x else lo)

    def onward(x, at, h, odd, band, action):
        source = unit(at, h, x)
        if x == 0:
            pl.when((at <= line) & has_up)(lambda: action(relay(source, band, UP, me + 4)))
            pl.when((at >= line) & has_down)(lambda: action(relay(source, band, DOWN, me - 4)))
            pl.when((at != skip) | (odd == 0))(
                lambda: action(relay(source, band, BESIDE, beside))
            )
        else:
            wanted = (at == mate_skip) & (odd == 1)
            pl.when(wanted & (mate > line))(lambda: action(relay(source, band, UP, me + 4)))
            pl.when(wanted & (mate < line))(lambda: action(relay(source, band, DOWN, me - 4)))

    def first_copies(action):
        for band in HAULS:
            action(first_copy(band, PARTNER, partner))
            pl.when(has_up)(lambda: action(first_copy(band, UP, me + 4)))
            pl.when(has_down)(lambda: action(first_copy(band, DOWN, me - 4)))
            action(first_copy(band, BESIDE, beside))

    def multiply(source, side, first, stop):
        tile_pair = (owner[KT_DEV * source], owner[KT_DEV * source + 1])
        home = partner if side else me
        rows = slice(first * PBLK, stop * PBLK)
        for slot, tile in enumerate(tile_pair):
            columns = slice(slot * TILE, (slot + 1) * TILE)
            for block in range(first, stop):
                part = slice(block * PBLK, (block + 1) * PBLK)
                value = gath[source, part, columns]
                for n in range(KT_DEV):
                    mark = screen[block, tile, KT_DEV * home + n].astype(jnp.float32)
                    lhs[n, part, columns] = value * jnp.full(value.shape, mark, jnp.float32).astype(
                        value.dtype
                    )
        if side:
            right = jnp.concatenate([far[KT_DEV * source], far[KT_DEV * source + 1]], axis=0)
        else:
            right = jnp.concatenate([panel[tile] for tile in tile_pair], axis=0)
        for n in range(KT_DEV):
            columns = slice(n * TILE, (n + 1) * TILE)
            place = slice((KT_DEV * side + n) * TILE, (KT_DEV * side + n + 1) * TILE)
            acc[rows, place] += jnp.dot(
                lhs[n, rows], right[:, columns], preferred_element_type=jnp.float32
            )

    first_copies(start)
    for step in range(1, pairs):
        panel_copy(step).start()
    acc[...] = jnp.zeros_like(acc)
    get_owner.wait()
    own_ints.wait()
    for step in range(1, pairs):
        panel_copy(step).wait_recv()

    def fill(source, _):
        if_holder(
            source, core,
            lambda: stage.__setitem__(source, panel[owner[KT_DEV * source + core % 2]]),
        )
        return 0

    def to_partner(action, first, stop):
        def body(level, _):
            def send(x, at, h, odd):
                source = unit(at, 1 - h, x)
                if_holder(source, core, lambda: action(far_copy(source)))

            on_level(level, send)
            return 0

        lax.fori_loop(first, stop, body, 0)

    def skipped_to_partner(action):
        source = unit(skip, hi, 1)
        if_holder(source, core, lambda: action(far_copy(source)))

    lax.fori_loop(0, ranks, fill, 0)
    to_partner(start, 0, 3)

    def pass_on(source):
        def go():
            far_copy(source).wait_recv()
            for step in range(1, pairs):
                pass_copy(source, step, core).start()

        if_holder(source, core, go)

    def passed(source):
        for step in range(1, pairs):
            holder = (core + step) % pairs
            if_holder(
                source, holder, lambda: pass_copy(source, step, holder).wait_recv()
            )

    def arrived(source, band):
        relay(source, band, BESIDE, beside).wait_recv()

    def far_whole(source):
        passed(source)
        multiply(source, 1, 0, blocks)

    def on_unit(action):
        return lambda x, at, h, odd: action(unit(at, h, x))

    def relay_level(level):
        for band in HAULS:

            def take(x, at, h, odd):
                arrived(unit(at, h, x), band)
                onward(x, at, h, odd, band, start)

            on_level(level, take)

    def near_level(level):
        on_level(level, on_unit(lambda source: multiply(source, 0, 0, blocks)))

    final = 2 * length + 1
    skipped_unit = unit(skip, 1 - hi, 1)
    outer = (line == 0) | (line == length - 1)
    lag = jnp.where(outer, 1, 2)

    def early_level(level, _):
        pl.when(level > 1)(lambda: relay_level(level))
        on_level(level - lag, on_unit(pass_on))
        near_level(level)
        on_level(level - lag - 1, on_unit(far_whole))
        return 0

    def late_level(level, _):
        on_level(level, on_unit(pass_on))
        relay_level(level)
        near_level(level)
        on_level(level - 1, on_unit(far_whole))
        return 0

    relay_level(1)
    to_partner(start, 3, 2 * length + 2)
    skipped_to_partner(start)
    get_screen.wait()
    own_amps.wait()
    multiply(me, 0, 0, blocks)
    lax.fori_loop(1, final - 2, early_level, 0)

    spot_in_plane = line * 2 + lo

    flips = [1 - 2 * lo, 2 * (1 - 2 * hi)]
    for bit in range(length.bit_length() - 1):
        flips.append((4 << bit) * (1 - 2 * ((line // (1 << bit)) % 2)))

    def moved(mask):
        return sum(flip for bit, flip in enumerate(flips) if mask >> bit & 1)

    def whole(buffer, count, send, recv):
        place = buffer.at[pl.ds(0, count)]
        return pltpu.make_async_remote_copy(
            src_ref=place, dst_ref=place, send_sem=send, recv_sem=recv,
            device_id={"vcol": beside}, device_id_type=MESH,
        )

    def send_slots(band):
        for mask in reversed(range(1, ranks)):
            target = me + moved(mask)
            pltpu.make_async_remote_copy(
                src_ref=slots[band].at[target], dst_ref=landed[band].at[me],
                send_sem=back_send.at[band], recv_sem=back_recv.at[band],
                device_id={"vcol": target}, device_id_type=MESH,
            ).start()

    def send_parts(side, band):
        for mask in reversed(range(1, ranks)):
            if mask & 2 == 0:
                target = me + moved(mask)
                column = spot_in_plane + moved(mask & 1) + moved(mask & -4) // 2
                pltpu.make_async_remote_copy(
                    src_ref=parts[band].at[side, column],
                    dst_ref=natural[band].at[
                        pl.ds((spot_in_plane * 2 + side) * KT_DEV, KT_DEV)
                    ],
                    send_sem=out_send.at[side, band], recv_sem=out_recv.at[band],
                    device_id={"vcol": target}, device_id_type=MESH,
                ).start()

    def parts_taken(band):
        return whole(
            natural[band], (plane - 1) * 2 * KT_DEV, out_send.at[0, band], out_recv.at[band]
        )

    def parts_sent(side, band):
        return whole(
            parts[band].at[side], plane - 1, out_send.at[side, band], out_recv.at[band]
        )

    def slots_moved(band):
        return whole(slots[band], ranks - 1, back_send.at[band], back_recv.at[band])

    def send_out(side, band):
        low, high = bands[band]
        part = (high - low) // plane
        for i in range(plane):
            for n in range(KT_DEV):
                column = (side * KT_DEV + n) * TILE
                parts[band][side, i, n] = acc[
                    low + i * part : low + (i + 1) * part, column : column + TILE
                ].astype(jnp.bfloat16)
        send_parts(side, band)
        natural[band][pl.ds((spot_in_plane * 2 + side) * KT_DEV, KT_DEV)] = parts[band][
            side, spot_in_plane
        ]

    @pl.when(outer)
    def _():
        on_level(final - 3, on_unit(pass_on))
        on_level(final - 4, on_unit(far_whole))
        lax.fori_loop(final - 2, final, late_level, 0)
        on_level(final, on_unit(pass_on))
        pass_on(skipped_unit)
        on_level(final - 1, on_unit(far_whole))
        on_level(final, on_unit(passed))
        passed(skipped_unit)
        for band in BANDS:
            low, high = bands[band]

            def finish(source):
                for haul, (top, _) in enumerate(hauls):
                    if low <= top < high:
                        arrived(source, haul)

            on_level(final, on_unit(finish))
            finish(skipped_unit)
            for side in (0, 1):
                part = functools.partial(
                    multiply, side=side, first=low // PBLK, stop=high // PBLK
                )
                on_level(final, on_unit(part))
                part(skipped_unit)
                send_out(side, band)

    @pl.when(~outer)
    def _():
        relay_level(final - 2)
        near_level(final - 2)
        for band in HAULS:
            arrived(skipped_unit, band)
        multiply(skipped_unit, 0, 0, blocks)
        for band in BANDS:
            send_out(0, band)

        def rest(level, _):
            on_level(level, on_unit(pass_on))
            on_level(level - 1, on_unit(far_whole))
            return 0

        on_level(final - 4, on_unit(pass_on))
        on_level(final - 5, on_unit(far_whole))
        lax.fori_loop(final - 3, final - 1, rest, 0)
        pass_on(skipped_unit)
        on_level(final - 2, on_unit(far_whole))
        passed(skipped_unit)
        for band in BANDS:
            low, high = bands[band]
            multiply(skipped_unit, 1, low // PBLK, high // PBLK)
            send_out(1, band)

    def find(slot, _):
        tile = owner[slot]
        row, col = (tile >> 2) & 1, (tile >> 1) & 1
        place[slot] = (tile & -8) | (col << 2) | ((row ^ hi) << 1) | (tile & 1)
        return 0

    lax.fori_loop(0, KT_DEV * ranks, find, 0)
    get_occ.wait()
    get_virt.wait()
    get_mine.wait()
    rows = mine.shape[0]
    eye = lax.broadcasted_iota(jnp.int32, (TILE, TILE), 0) == lax.broadcasted_iota(
        jnp.int32, (TILE, TILE), 1
    )
    for g in range(rows // TILE):
        part = slice(g * TILE, (g + 1) * TILE)
        spread = jnp.broadcast_to(occ[g : g + 1, :], (TILE, TILE))
        column = jnp.sum(jnp.where(eye, spread, 0.0), axis=1, keepdims=True)
        for n in range(KT_DEV):
            columns = slice(n * TILE, (n + 1) * TILE)
            level = virt[pl.ds(owner[KT_DEV * me + n], 1), :]
            base[part, columns] = (level - column) * mine[part, columns].astype(jnp.float32)

    for band in BANDS:
        parts_taken(band).wait_recv()
        for j in range(ranks):
            for n in range(KT_DEV):
                slots[band][j, n] = natural[band][place[KT_DEV * j + n]]
        send_slots(band)
        landed[band][me] = slots[band][me]

    first_copies(wait_send)

    def drain(level, _):
        for band in HAULS:
            on_level(
                level, lambda x, at, h, odd: onward(x, at, h, odd, band, wait_send)
            )
        return 0

    lax.fori_loop(1, final + 1, drain, 0)
    to_partner(wait_send, 0, 2 * length + 2)
    skipped_to_partner(wait_send)

    def close(source, _):
        def go():
            for step in range(1, pairs):
                pass_copy(source, step, core).wait_send()

        if_holder(source, core, go)
        return 0

    lax.fori_loop(0, ranks, close, 0)
    for step in range(1, pairs):
        panel_copy(step).wait_send()
    for band in BANDS:
        for side in (0, 1):
            parts_sent(side, band).wait_send()

    for band in BANDS:
        low, high = bands[band]
        part = (high - low) // plane
        slots_moved(band).wait_recv()
        for j in range(ranks):
            at = ((j % 4) // 2) * half + low + ((j // 4) * 2 + j % 2) * part
            for n in range(KT_DEV):
                columns = slice(n * TILE, (n + 1) * TILE)
                out[at : at + part, columns] = (
                    landed[band][j, n].astype(jnp.float32) + base[at : at + part, columns]
                ).astype(out.dtype)
    for band in BANDS:
        slots_moved(band).wait_send()


def local(ranks, pairs, amplitudes, tile_owner, integrals, screening, occ_energy, virt_energy):
    rows, width = amplitudes.shape
    tiles = integrals.shape[0] // TILE
    count = tile_owner.shape[0]
    half, plane = rows // 2, ranks // 2
    blocks = half // PBLK
    hbm = pl.BlockSpec(memory_space=pl.ANY)
    dma = pltpu.SemaphoreType.DMA
    sizes = [(high - low) // plane for low, high in band_edges(half, SHARES)]

    def exchange(lead):
        return [pltpu.VMEM((*lead, size, TILE), jnp.bfloat16) for size in sizes]

    return pl.pallas_call(
        functools.partial(ladder_kernel, ranks, pairs),
        out_shape=pltpu.VMEM((rows, width), jnp.bfloat16),
        in_specs=[hbm] * 6,
        out_specs=pl.BlockSpec(memory_space=pltpu.VMEM),
        scratch_shapes=[
            pltpu.SMEM((count,), jnp.int32),
            pltpu.SMEM((count,), jnp.int32),
            pltpu.SMEM((blocks, count, count), jnp.int32),
            pltpu.VMEM((rows // TILE, TILE), jnp.float32),
            pltpu.VMEM((count, TILE), jnp.float32),
            pltpu.VMEM((rows, width), jnp.bfloat16),
            pltpu.VMEM((rows, width), jnp.float32),
            pltpu.VMEM((ranks, half, width), jnp.bfloat16),
            pltpu.VMEM((tiles * pairs, TILE, width), jnp.bfloat16),
            pltpu.VMEM((ranks, TILE, width), jnp.bfloat16),
            pltpu.VMEM((KT_DEV * ranks, TILE, width), jnp.bfloat16),
            pltpu.VMEM((KT_DEV, half, width), jnp.bfloat16),
            pltpu.VMEM((half, 2 * width), jnp.float32),
            exchange((2, plane, KT_DEV)),
            exchange((plane * 2 * KT_DEV,)),
            exchange((ranks, KT_DEV)),
            exchange((ranks, KT_DEV)),
            dma((7,)),
            dma((len(HAULS), 4, ranks)),
            dma((len(HAULS), ranks)),
            dma((pairs - 1,)),
            dma((pairs - 1,)),
            dma((ranks,)),
            dma((ranks,)),
            dma((pairs - 1, KT_DEV * ranks)),
            dma((KT_DEV * ranks,)),
            dma((2, len(BANDS))),
            dma((len(BANDS),)),
            dma((len(BANDS),)),
            dma((len(BANDS),)),
        ],
        compiler_params=pltpu.CompilerParams(
            collective_id=0, has_side_effects=True, vmem_limit_bytes=62 * 1024 * 1024
        ),
    )(
        amplitudes,
        tile_owner,
        integrals.reshape(tiles, TILE, width),
        screening,
        occ_energy.reshape(rows // TILE, TILE),
        virt_energy.reshape(count, TILE),
    )


def solution(mesh):
    return jax.shard_map(
        functools.partial(local, mesh.shape["vcol"], mesh.shape["pair"]),
        mesh=mesh,
        in_specs=(P("pair", "vcol"), P(), P("pair", "vcol"), P("pair", None, None), P("pair"), P()),
        out_specs=P("pair", "vcol"),
        check_vma=False,
    )
```
